32 devices in a mesh: band: 4 (over y, core), pw: 8 (over z, x).
Axes of the slice: x: 2, y: 2, z: 4, core: 2. Of those that a mesh axis runs over, the one named last changes fastest.
Arguments:
- response: bfloat16 [4, 2, 62464], P('band', None, 'pw'), may hold values from -6 to 6
- panel: bfloat16 [256, 2, 62464], P('band', None, 'pw'), may hold values from -0.0234375 to 0.0234375
- energies: float32 [256], replicated, may hold values from -1 to 0
- offset: int32 [1], replicated, may hold values from 0 to 252
- grid_map: int32 [62464], P('pw'), may hold values from 0 to 511999, as said below
- potential: float32 [160, 160, 160], P(None, 'pw'), may hold values from -6 to 2
- contact: float32 [160, 160, 160], P(None, 'pw'), may hold values from -10240 to 10240
Outputs:
- residual: bfloat16 [4, 2, 62464], P('band', None, 'pw')
- response_next: bfloat16 [4, 2, 62464], P('band', None, 'pw')
The draws below stay inside these ranges and needn't reach their ends.
Inputs may be any that keep to these rules, and one draw needn't show every extreme that they name: `grid_map`: within each aligned block of 7808 entries (the plane waves of block p) the entries are distinct cells lx * 160 * 160 + ly * 160 + lz of the 20 grid planes gx = p + lx * 8; they are the 7808 cells of those planes with the smallest fx^2 + fy^2 + fz^2 in folded coordinates, ties among equal radii taken in any way.
All inputs are finite; a program needn't handle non-finite values.
Results may differ from the reference program's by a relative error of at most 0.015.
Values may be sent and summed in bfloat16 or wider, within the bound.
No kernel may reach another device: no remote copies, remote signals or barrier semaphores. Data moves between devices by JAX's collectives and lax.ppermute only.
A program may use at most 256 MiB of HBM per device.

```python
import math
import jax
import jax.numpy as jnp
from jax import lax

NG = 160
OCC_DEV = 64
NPW_DEV = 7808
SLAB = 20
NB = 4
NOCC = 256
NPW = 62464


def draw_grid_map(key, part):
    cell_count = SLAB * NG * NG
    block_count = NPW // NPW_DEV
    cells = jnp.arange(cell_count, dtype=jnp.int32)
    local_x = cells // (NG * NG)
    coord_y = cells // NG % NG
    coord_z = cells % NG

    def folded_square(coord):
        folded = jnp.where(coord >= NG // 2, coord - NG, coord)
        return folded * folded

    def one_block(block_index, block_key):
        first_key, second_key = jax.random.split(block_key)
        coord_x = block_index + block_count * local_x
        radius = folded_square(coord_x) + folded_square(coord_y) + folded_square(coord_z)
        shuffle = jax.random.permutation(first_key, cell_count).astype(jnp.int32)
        order = jnp.argsort(radius[shuffle], stable=True)[:NPW_DEV]
        chosen = shuffle[order].astype(jnp.int32)
        return jax.random.permutation(second_key, chosen).astype(jnp.int32)
    block_keys = jax.random.split(jax.random.fold_in(key, 7), block_count)
    block_ids = jnp.arange(block_count, dtype=jnp.int32)
    return jax.vmap(one_block)(block_ids, block_keys).reshape(-1).astype(jnp.int32)


def levels(stream_key, shape, cuts, least, top_value):
    def one(dim, shards_of):
        heights = jax.random.uniform(jax.random.fold_in(jax.random.fold_in(stream_key, 6), dim), (shards_of,), jnp.float32, least / len(cuts), top_value / len(cuts))
        return jnp.repeat(jnp.exp(heights), shape[dim] // shards_of).reshape((-1,) + (1,) * (len(shape) - dim - 1))

    factor_of = one(*cuts[0])
    for cut in cuts[1:]:
        factor_of = factor_of * one(*cut)
    return factor_of


def bell_draw(key, shape, deviation, most, cuts=(), kind=jnp.bfloat16):
    values = jax.random.normal(key, shape, jnp.float32) * deviation
    if len(cuts) > 0:
        values = levels(key, shape, cuts, -0.22, 0.18) * values
    return jnp.clip(values, min=-most, max=most).astype(kind)


def setup_inputs(seed: int = 0) -> dict:
    arg_keys = jax.random.split(jax.random.key(seed), 8)
    response = bell_draw(arg_keys[0], (NB, 2, NPW), 1.0, 6.0, ((0, 4), (2, 8)))
    panel = bell_draw(arg_keys[1], (NOCC, 2, NPW), NPW ** -0.5, 0.0234375, ((0, 4), (2, 8)))
    energies = jnp.clip(jax.random.uniform(arg_keys[2], (NOCC,), jnp.float32, -1.0, 0.0), -1.0, 0.0)
    offset = jax.random.randint(arg_keys[3], (1,), 0, NOCC - NB + 1).astype(jnp.int32)
    grid_map = draw_grid_map(jax.random.fold_in(arg_keys[7], 71), 0)
    potential = jnp.clip(-6.0 + 8.0 * jax.random.uniform(arg_keys[5], (NG, NG, NG), jnp.float32) ** levels(arg_keys[5], (NG, NG, NG), ((1, 8),), -0.2, 0.2), -6.0, 2.0)
    contact = bell_draw(arg_keys[6], (NG, NG, NG), (NG * NG // 16), 10240.0, ((1, 8),), jnp.float32)
    return {"response": response, "panel": panel, "energies": energies, "offset": offset, "grid_map": grid_map, "potential": potential, "contact": contact}


def fourier_table(length, sign_value):
    indices = jnp.arange(length, dtype=jnp.int32)
    products = indices[:, None] * indices[None, :] % length
    angles = products.astype(jnp.float32) * (2.0 * math.pi / length)
    scaling = 1.0 / math.sqrt(length)
    cosine = jnp.cos(angles) * scaling
    sine_part = sign_value * jnp.sin(angles) * scaling
    factor = jnp.stack([jnp.stack([cosine, sine_part]), jnp.stack([-sine_part, cosine])])
    return factor.astype(jnp.bfloat16)

def along_z(field, factor):
    return jnp.einsum('bcxyk,cdkw->bdxyw', field.astype(jnp.float32), factor.astype(jnp.float32))

def along_y(field, factor):
    return jnp.einsum('bcxky,cdkw->bdxwy', field.astype(jnp.float32), factor.astype(jnp.float32))

def along_x(field, factor):
    return jnp.einsum('bckyz,cdkw->bdwyz', field.astype(jnp.float32), factor.astype(jnp.float32))

def folded_square(coord):
    half_grid = NG // 2
    folded = jnp.where(coord >= half_grid, coord - NG, coord)
    return folded * folded

def swapped_terms(terms):
    other = jnp.stack([terms[:, 1], -terms[:, 0]], axis=1)
    return jnp.stack([terms, other]).astype(jnp.float32)

def reference(response, panel, energies, offset, grid_map, potential, contact):
    first_row = offset[0]
    partner = lax.dynamic_slice_in_dim(panel, first_row, NB, 0)
    shifts = lax.dynamic_slice_in_dim(energies, first_row, NB, 0)
    owner = jnp.arange(NPW, dtype=jnp.int32) // NPW_DEV
    grid_x = owner + NPW // NPW_DEV * (grid_map // (NG * NG))
    grid_y = grid_map // NG % NG
    grid_z = grid_map % NG
    squares = folded_square(grid_x) + folded_square(grid_y) + folded_square(grid_z)
    kinetic = 1.5 * squares.astype(jnp.float32) / float(NG // 2 * (NG // 2))
    flat_cells = (grid_x * NG + grid_y) * NG + grid_z
    own_term = ((kinetic[None, None, :] - shifts[:, None, None]) * response.astype(jnp.float32)).astype(jnp.bfloat16)
    forward = fourier_table(NG, 1.0)
    backward = fourier_table(NG, -1.0)

    def one_band(pair):
        coeffs = jnp.stack([pair[0], pair[1]])
        flat = jnp.zeros((2, 2, NG * NG * NG), jnp.bfloat16).at[:, :, flat_cells].set(coeffs)
        field = flat.reshape(2, 2, NG, NG, NG)
        field = along_z(field, forward).astype(jnp.bfloat16)
        field = along_y(field, forward).astype(jnp.bfloat16)
        field = along_x(field, forward).astype(jnp.bfloat16)
        mixed_field = (potential * field[0].astype(jnp.float32) + contact * field[1].astype(jnp.float32)).astype(jnp.bfloat16)
        back_field = along_x(mixed_field[None], backward).astype(jnp.bfloat16)
        back_field = along_y(back_field, backward).astype(jnp.bfloat16)
        back_field = along_z(back_field, backward)
        return back_field.reshape(2, NG * NG * NG)[:, flat_cells].astype(jnp.bfloat16)
    field_term = lax.map(one_band, (response, partner))
    own_swapped = swapped_terms(own_term)
    field_swapped = swapped_terms(field_term)
    blocks = panel.reshape(NOCC // OCC_DEV, OCC_DEV, 2, NPW)

    def block_correlation(rows):
        rows_wide = rows.astype(jnp.float32)
        return jnp.einsum('mcj,dncj->dmn', rows_wide, own_swapped) + jnp.einsum('mcj,dncj->dmn', rows_wide, field_swapped)
    pieces = lax.map(block_correlation, blocks)
    correlation = jnp.moveaxis(pieces, 0, 1).reshape(2, NOCC, NB)
    correlation_low = correlation.astype(jnp.bfloat16)
    spread = jnp.stack([jnp.stack([correlation_low[0], -correlation_low[1]]), jnp.stack([correlation_low[1], correlation_low[0]])])
    spread_blocks = jnp.moveaxis(spread.reshape(2, 2, NOCC // OCC_DEV, OCC_DEV, NB), 2, 0)

    def add_block(carry, inputs):
        rows, weights = inputs
        term = jnp.einsum('mcj,dcmn->ndj', rows.astype(jnp.float32), weights.astype(jnp.float32))
        return (carry + term, None)
    correction, unused = lax.scan(add_block, jnp.zeros((NB, 2, NPW), jnp.float32), (blocks, spread_blocks))
    summed = own_term.astype(jnp.float32) + field_term.astype(jnp.float32) - correction
    residual = summed.astype(jnp.bfloat16)
    response_next = (response.astype(jnp.float32) - summed / (1.0 + kinetic)[None, None, :]).astype(jnp.bfloat16)
    return (residual, response_next)
```

```python
import functools
import math

import jax
import jax.numpy as jnp
import numpy as np
from jax import lax
from jax.experimental import pallas as pl
from jax.experimental.pallas import tpu as pltpu
from jax.sharding import PartitionSpec as P

F32, BF16, I32 = jnp.float32, jnp.bfloat16, jnp.int32


def up(value, step):
    return -(-value // step) * step


class Box:
    def __init__(self, grid, blocks, count):
        self.grid, self.blocks, self.count = grid, blocks, count
        self.slab = grid // blocks
        folded = np.arange(grid)
        folded = np.where(folded >= grid // 2, folded - grid, folded)
        flat = np.sort((folded[:, None] ** 2 + folded[None, :] ** 2).ravel())
        used, half = set(), 0
        for block in range(blocks):
            planes = folded[block + blocks * np.arange(self.slab)] ** 2
            radii = np.sort((planes[:, None] + flat[None, :]).ravel())
            limit = int(radii[count - 1])
            used |= set(np.nonzero(planes <= limit)[0].tolist())
            half = max(half, math.isqrt(limit - int(planes.min())))
        self.low = 0
        while self.low in used and self.low < self.slab:
            self.low += 1
        self.slots = self.low + len([u for u in used if u >= self.low])
        if any(u in used for u in range(self.low, self.slab - (self.slots - self.low))):
            self.low = self.slots = self.slab
        self.planes = [s if s < self.low else s + self.slab - self.slots for s in range(self.slots)]
        self.half = min(half, grid // 2 - 1) if 2 * half + 1 <= grid else grid // 2
        self.width = min(2 * self.half + 1, grid)
        self.ypad = up(self.width, 8)
        self.zpad = 64 if self.width <= 64 else up(self.width, 128)
        self.rows = up(self.slots * self.slab, 16)
        self.spad = self.slots
        while self.spad * self.slab % 8 or self.spad * self.slab < self.rows:
            self.spad += 1

    def waves(self, first, other):
        products = (np.asarray(first)[:, None] * np.asarray(other)[None, :]) % self.grid
        angles = products.astype(np.float32) * np.float32(2.0 * math.pi / self.grid)
        scaling = np.float32(1.0 / math.sqrt(self.grid))
        return np.cos(angles) * scaling, np.sin(angles) * scaling

    def tables(self):
        grid, ypad, zpad = self.grid, self.ypad, self.zpad
        every = np.arange(grid)
        boxed = np.arange(self.width) - self.half

        def padded(part, rows, columns):
            return np.pad(part, ((0, rows - part.shape[0]), (0, columns - part.shape[1])))

        cos_y, sin_y = self.waves(every, boxed)
        up_y = np.concatenate([padded(cos_y, grid, ypad), padded(sin_y, grid, ypad)], 1)
        down_y = np.concatenate([padded(cos_y.T, ypad, grid), padded(-sin_y.T, ypad, grid)], 0)
        cos_z, sin_z = padded(cos_y, grid, zpad), padded(sin_y, grid, zpad)
        up_z = np.stack([np.concatenate([cos_z.T, -sin_z.T], 0), np.concatenate([sin_z.T, cos_z.T], 0)])
        down_z = np.stack([np.concatenate([cos_z, -sin_z], 1), np.concatenate([sin_z, cos_z], 1)])
        planes = np.array([p + self.blocks * x for p in range(self.blocks) for x in self.planes])
        cos_x, sin_x = self.waves(every, planes)

        def slotted(part):
            part = part.reshape(grid, self.blocks, self.slots)
            part = np.pad(part, ((0, 0), (0, 0), (0, self.spad - self.slots)))
            return part.reshape(grid, self.blocks * self.spad)

        cos_x, sin_x = slotted(cos_x), slotted(sin_x)
        up_x = np.concatenate([cos_x, sin_x], 1)
        down_x = np.concatenate([cos_x.T, -sin_x.T], 0)
        return [jnp.asarray(t, BF16) for t in (up_y, down_y, up_x, down_x, up_z, down_z)]


def quarter(field, zpad):
    pieces = []
    for start in range(0, field.shape[1], 2 * zpad):
        piece = field[:, start : start + 2 * zpad]
        if 2 * zpad == 128:
            lane = lax.broadcasted_iota(I32, piece.shape, 1)
            turned = pltpu.roll(piece, zpad, 1)
            pieces.append(jnp.where(lane < zpad, -turned, turned))
        else:
            pieces += [-piece[:, zpad:], piece[:, :zpad]]
    return pieces[0] if len(pieces) == 1 else jnp.concatenate(pieces, 1)


def chunks(total, step):
    return [(start, min(step, total - start)) for start in range(0, total, step)]


def dot(left, right, dims=((1,), (0,))):
    return lax.dot_general(left, right, (dims, ((), ())), preferred_element_type=F32)


def pick_rows(rows, index):
    return lax.broadcasted_iota(I32, (rows, index.shape[1]), 0) == index


def scatter_kernel(box, row_ref, z_ref, resp_ref, part_ref, up_y_ref, out_ref, space_ref):
    zpad, ypad, slab = box.zpad, box.ypad, box.slab
    total = None
    for start, size in chunks(box.count, 1024):
        span = slice(start, start + size)
        chosen = jnp.where(pick_rows(box.slots * ypad, row_ref[:, span]), 1.0, 0.0).astype(BF16)
        at_z = pick_rows(zpad, z_ref[:, span])
        values = []
        for ref in (resp_ref, part_ref):
            pair = ref[0, :, span].astype(F32)
            values += [jnp.where(at_z, pair[c : c + 1], 0.0).astype(BF16) for c in range(2)]
        piece = dot(chosen, jnp.concatenate(values, 0), ((1,), (1,)))
        total = piece if total is None else total + piece
    for s in range(box.slots):
        plane = total[s * ypad : (s + 1) * ypad]
        both = jnp.concatenate([plane, quarter(plane, zpad)], 0).astype(BF16)
        lines = dot(up_y_ref[...], both)
        for q in range(box.blocks):
            space_ref[q, s * slab : (s + 1) * slab, :] = lines[q * slab : (q + 1) * slab]
    used = box.slots * slab
    for q in range(box.blocks):
        if used < box.rows:
            space_ref[q, used:, :] = jnp.zeros((box.rows - used, space_ref.shape[2]), F32)
        out_ref[q] = space_ref[q].astype(BF16)


def mix_kernel(
    box, lines, in_ref, pot_ref, con_ref, up_x_ref, down_x_ref, up_z_ref, down_z_ref, out_ref, from_ref, to_ref
):
    zpad, slab, stride = box.zpad, box.slab, box.spad * box.slab
    planes, tiles = box.blocks * box.spad, 2 * zpad // 128
    step = pl.program_id(0)

    @pl.when(step == 0)
    def _():
        for p in range(box.blocks):
            for t in range(2 * tiles):
                from_ref[t, p * stride : p * stride + box.rows, :] = in_ref[
                    p, :, t * 128 : (t + 1) * 128
                ].astype(F32)
                if box.rows < stride:
                    from_ref[t, p * stride + box.rows : (p + 1) * stride, :] = jnp.zeros(
                        (stride - box.rows, 128), F32
                    )

    for i in range(lines):
        line = step * lines + i
        space = []
        for f in range(2):
            plane = jnp.concatenate(
                [
                    from_ref[f * tiles + t, pl.ds(line, planes, stride=slab), :]
                    for t in range(tiles)
                ],
                1,
            )
            both = jnp.concatenate([plane, quarter(plane, zpad)], 0).astype(BF16)
            wide = dot(up_x_ref[...], both).astype(BF16)
            space.append([dot(wide, up_z_ref[d]) for d in range(2)])
        potential, contact = pot_ref[i], con_ref[i]
        mixed = [(potential * space[0][d] + contact * space[1][d]).astype(BF16) for d in range(2)]
        back = (dot(mixed[0], down_z_ref[0]) + dot(mixed[1], down_z_ref[1])).astype(BF16)
        parts = dot(down_x_ref[...], back)
        lined = parts[:planes] + quarter(parts[planes:], zpad)
        for t in range(tiles):
            to_ref[t, pl.ds(line, planes, stride=slab), :] = lined[:, t * 128 : (t + 1) * 128]

    @pl.when(step == pl.num_programs(0) - 1)
    def _():
        for p in range(box.blocks):
            for t in range(tiles):
                out_ref[p, :, t * 128 : (t + 1) * 128] = to_ref[
                    t, p * stride : p * stride + box.rows, :
                ].astype(BF16)


def term_kernel(
    box, in_ref, row_ref, z_ref, resp_ref, factor_ref, down_y_ref, low_ref, term_ref, space_ref
):
    zpad, ypad, slab = box.zpad, box.ypad, box.slab
    for q in range(box.blocks):
        space_ref[q] = in_ref[q].astype(F32)
    fields = []
    for s in range(box.slots):
        plane = jnp.concatenate(
            [space_ref[q, s * slab : (s + 1) * slab, :] for q in range(box.blocks)], 0
        ).astype(BF16)
        parts = dot(down_y_ref[...], plane)
        fields.append(parts[:ypad] + quarter(parts[ypad:], zpad))
    field = jnp.concatenate(fields, 0).T.astype(BF16)
    for start, size in chunks(box.count, 1024):
        span = slice(start, start + size)
        chosen = jnp.where(pick_rows(box.slots * ypad, row_ref[:, span]), 1.0, 0.0).astype(BF16)
        at_z = pick_rows(zpad, z_ref[:, span])
        found = dot(field, chosen)
        pair = resp_ref[0, :, span].astype(F32)
        rows = []
        for c in range(2):
            value = jnp.sum(jnp.where(at_z, found[c * zpad : (c + 1) * zpad], 0.0), 0, keepdims=True)
            own = (factor_ref[:, span] * pair[c : c + 1]).astype(BF16).astype(F32)
            rows.append(own + value)
        both = jnp.concatenate(rows, 0)
        term_ref[0, :, span] = both
        low_ref[0, :, span] = both.astype(BF16)


def whole_call(kernel, out_shape, scratch, args, cost):
    return pl.pallas_call(
        kernel,
        out_shape=out_shape,
        in_specs=[pl.BlockSpec(memory_space=pltpu.VMEM)] * len(args),
        out_specs=jax.tree.map(lambda _: pl.BlockSpec(memory_space=pltpu.VMEM), out_shape),
        scratch_shapes=scratch,
        compiler_params=pltpu.CompilerParams(vmem_limit_bytes=48 << 20),
        cost_estimate=pl.CostEstimate(flops=cost, bytes_accessed=1 << 20, transcendentals=0),
    )(*args)


def mix_call(box, received, potential, contact, tables):
    grid, slab = box.grid, box.slab
    steps = 5 if slab % 5 == 0 else slab
    lines = slab // steps
    full = lambda shape: pl.BlockSpec(shape, lambda g: (0,) * len(shape))
    height = box.blocks * box.spad * slab
    block = pl.BlockSpec((lines, grid, grid), lambda g: (g, 0, 0))
    return pl.pallas_call(
        functools.partial(mix_kernel, box, lines),
        out_shape=jax.ShapeDtypeStruct((box.blocks, box.rows, 2 * box.zpad), BF16),
        grid=(steps,),
        in_specs=[full(received.shape), block, block] + [full(t.shape) for t in tables],
        out_specs=full((box.blocks, box.rows, 2 * box.zpad)),
        scratch_shapes=[
            pltpu.VMEM((2 * box.zpad // 64, height, 128), F32),
            pltpu.VMEM((2 * box.zpad // 128, height, 128), F32),
        ],
        compiler_params=pltpu.CompilerParams(
            vmem_limit_bytes=48 << 20, dimension_semantics=("arbitrary",)
        ),
        cost_estimate=pl.CostEstimate(flops=1 << 32, bytes_accessed=8 << 20, transcendentals=0),
    )(received, potential, contact, *tables)


def folded_square(coord, grid_size):
    folded = jnp.where(coord >= grid_size // 2, coord - grid_size, coord)
    return folded * folded


def on_device(sizes, response, panel, energies, offset, grid_map, potential, contact):
    rows_here, count = panel.shape[0], grid_map.shape[0]
    grid = potential.shape[0]
    bands, blocks = sizes
    box = Box(grid, blocks, count)
    up_y, down_y, up_x, down_x, up_z, down_z = box.tables()
    band_me = lax.axis_index("band")
    first_row = offset[0]

    local = first_row - band_me * rows_here
    picked = jnp.concatenate(
        [
            lax.dynamic_slice_in_dim(panel, jnp.clip(local + n, 0, rows_here - 1), 1, 0)
            for n in range(bands)
        ],
        0,
    )
    arrived = lax.all_to_all(picked, "band", split_axis=0, concat_axis=0, tiled=True)
    owner = (first_row + band_me) // rows_here
    partner = lax.dynamic_slice_in_dim(arrived, owner, 1, 0)
    shift = lax.dynamic_slice_in_dim(energies, first_row + band_me, 1, 0)

    plane_size = grid * grid
    local_x = grid_map // plane_size
    grid_x = lax.axis_index("pw") + blocks * local_x
    grid_y = grid_map // grid % grid
    grid_z = grid_map % grid
    squares = folded_square(grid_x, grid) + folded_square(grid_y, grid) + folded_square(grid_z, grid)
    kinetic = 1.5 * squares.astype(F32) / float(grid // 2 * (grid // 2))
    slot = jnp.where(local_x < box.low, local_x, local_x - (box.slab - box.slots))
    row_index = (slot * box.ypad + (grid_y + box.half) % grid)[None, :]
    z_index = ((grid_z + box.half) % grid)[None, :]
    factor = (kinetic - shift[0])[None, :]

    sent = whole_call(
        functools.partial(scatter_kernel, box),
        jax.ShapeDtypeStruct((blocks, box.rows, 4 * box.zpad), BF16),
        [pltpu.VMEM((blocks, box.rows, 4 * box.zpad), F32)],
        (row_index, z_index, response, partner, up_y),
        1 << 32,
    )
    received = lax.all_to_all(sent, "pw", split_axis=0, concat_axis=0, tiled=True)
    returned = mix_call(
        box,
        received,
        jnp.transpose(potential, (1, 0, 2)),
        jnp.transpose(contact, (1, 0, 2)),
        (up_x, down_x, up_z, down_z),
    )
    combed = lax.all_to_all(returned, "pw", split_axis=0, concat_axis=0, tiled=True)
    term_low, term = whole_call(
        functools.partial(term_kernel, box),
        (
            jax.ShapeDtypeStruct((1, 2, count), BF16),
            jax.ShapeDtypeStruct((1, 2, count), F32),
        ),
        [pltpu.VMEM((blocks, box.rows, 2 * box.zpad), F32)],
        (combed, row_index, z_index, response, factor, down_y),
        1 << 32,
    )

    terms = lax.all_gather(term_low, "band", axis=0, tiled=True)
    other = jnp.stack([terms[:, 1], -terms[:, 0]], axis=1)
    swapped = jnp.stack([terms, other])
    correlation = jnp.einsum("mcj,dncj->dmn", panel, swapped, preferred_element_type=F32)
    near = 1
    while near < blocks:
        pairs = [(source, source ^ near) for source in range(blocks)]
        correlation = correlation + lax.ppermute(correlation, "pw", pairs)
        near *= 2
    low = correlation.astype(BF16)
    spread = jnp.stack([jnp.stack([low[0], -low[1]]), jnp.stack([low[1], low[0]])])
    shares = jnp.einsum("mcj,dcmn->ndj", panel, spread, preferred_element_type=F32).astype(BF16)
    parts = lax.all_to_all(shares, "band", split_axis=0, concat_axis=0, tiled=True)
    correction = jnp.sum(parts.astype(F32), axis=0, keepdims=True)
    summed = term - correction
    residual = summed.astype(BF16)
    response_next = (response.astype(F32) - summed / (1.0 + kinetic)[None, None, :]).astype(BF16)
    return (residual, response_next)


def solution(mesh):
    return jax.shard_map(
        functools.partial(on_device, (mesh.shape["band"], mesh.shape["pw"])),
        mesh=mesh,
        in_specs=(
            P("band", None, "pw"),
            P("band", None, "pw"),
            P(),
            P(),
            P("pw"),
            P(None, "pw", None),
            P(None, "pw", None),
        ),
        out_specs=(P("band", None, "pw"), P("band", None, "pw")),
        check_vma=False,
    )
```

```python
import functools
import math

import jax
import jax.numpy as jnp
import numpy as np
from jax import lax
from jax.experimental import pallas as pl
from jax.experimental.layout import Layout, with_layout_constraint
from jax.experimental.pallas import tpu as pltpu
from jax.sharding import PartitionSpec as P

F32, BF16, I32 = jnp.float32, jnp.bfloat16, jnp.int32


def up(value, step):
    return -(-value // step) * step


class Box:
    def __init__(self, grid, blocks, count):
        self.grid, self.blocks, self.count = grid, blocks, count
        self.slab = grid // blocks
        folded = np.arange(grid)
        folded = np.where(folded >= grid // 2, folded - grid, folded)
        flat = np.sort((folded[:, None] ** 2 + folded[None, :] ** 2).ravel())
        used, half = set(), 0
        for block in range(blocks):
            planes = folded[block + blocks * np.arange(self.slab)] ** 2
            radii = np.sort((planes[:, None] + flat[None, :]).ravel())
            limit = int(radii[count - 1])
            used |= set(np.nonzero(planes <= limit)[0].tolist())
            half = max(half, math.isqrt(limit - int(planes.min())))
        self.low = 0
        while self.low in used and self.low < self.slab:
            self.low += 1
        self.slots = self.low + len([u for u in used if u >= self.low])
        if any(u in used for u in range(self.low, self.slab - (self.slots - self.low))):
            self.low = self.slots = self.slab
        self.planes = [s if s < self.low else s + self.slab - self.slots for s in range(self.slots)]
        self.half = min(half, grid // 2 - 1) if 2 * half + 1 <= grid else grid // 2
        self.width = min(2 * self.half + 1, grid)
        self.ypad = up(self.width, 8)
        self.zpad = 64 if self.width <= 64 else up(self.width, 128)
        self.rows = up(self.slots * self.slab, 16)
        self.spad = self.slots
        while self.spad * self.slab % 8 or self.spad * self.slab < self.rows:
            self.spad += 1

    def waves(self, first, other):
        products = (np.asarray(first)[:, None] * np.asarray(other)[None, :]) % self.grid
        angles = products.astype(np.float32) * np.float32(2.0 * math.pi / self.grid)
        scaling = np.float32(1.0 / math.sqrt(self.grid))
        return np.cos(angles) * scaling, np.sin(angles) * scaling

    def tables(self):
        grid, ypad, zpad = self.grid, self.ypad, self.zpad
        every = np.arange(grid)
        boxed = np.arange(self.width) - self.half

        def padded(part, rows, columns):
            return np.pad(part, ((0, rows - part.shape[0]), (0, columns - part.shape[1])))

        cos_y, sin_y = self.waves(every, boxed)
        up_y = np.concatenate([padded(cos_y, grid, ypad), padded(sin_y, grid, ypad)], 1)
        down_y = np.concatenate([padded(cos_y.T, ypad, grid), padded(-sin_y.T, ypad, grid)], 0)
        cos_z, sin_z = padded(cos_y, grid, zpad), padded(sin_y, grid, zpad)
        up_z = np.stack([np.concatenate([cos_z.T, -sin_z.T], 0), np.concatenate([sin_z.T, cos_z.T], 0)])
        down_z = np.stack([np.concatenate([cos_z, -sin_z], 1), np.concatenate([sin_z, cos_z], 1)])
        planes = np.array([p + self.blocks * x for p in range(self.blocks) for x in self.planes])
        cos_x, sin_x = self.waves(every, planes)

        def slotted(part):
            part = part.reshape(grid, self.blocks, self.slots)
            part = np.pad(part, ((0, 0), (0, 0), (0, self.spad - self.slots)))
            return part.reshape(grid, self.blocks * self.spad)

        cos_x, sin_x = slotted(cos_x), slotted(sin_x)
        up_x = np.concatenate([cos_x, sin_x], 1)
        down_x = np.concatenate([cos_x.T, -sin_x.T], 0)
        return [jnp.asarray(t, BF16) for t in (up_y, down_y, up_x, down_x, up_z, down_z)]


def quarter(field, zpad):
    pieces = []
    for start in range(0, field.shape[1], 2 * zpad):
        piece = field[:, start : start + 2 * zpad]
        if 2 * zpad == 128:
            lane = lax.broadcasted_iota(I32, piece.shape, 1)
            turned = pltpu.roll(piece, zpad, 1)
            pieces.append(jnp.where(lane < zpad, -turned, turned))
        else:
            pieces += [-piece[:, zpad:], piece[:, :zpad]]
    return pieces[0] if len(pieces) == 1 else jnp.concatenate(pieces, 1)


def chunks(total, step):
    return [(start, min(step, total - start)) for start in range(0, total, step)]


def dot(left, right, dims=((1,), (0,))):
    return lax.dot_general(left, right, (dims, ((), ())), preferred_element_type=F32)


def pick_rows(rows, index):
    return lax.broadcasted_iota(I32, (rows, index.shape[1]), 0) == index


def scattered(box, row_ref, z_ref, value_ref, up_y_ref, out_ref, space_ref):
    zpad, ypad, slab = box.zpad, box.ypad, box.slab
    total = None
    for start, size in chunks(box.count, 1024):
        span = slice(start, start + size)
        chosen = jnp.where(pick_rows(box.slots * ypad, row_ref[:, span]), 1.0, 0.0).astype(BF16)
        at_z = pick_rows(zpad, z_ref[:, span])
        pair = value_ref[0, :, span].astype(F32)
        values = [jnp.where(at_z, pair[c : c + 1], 0.0).astype(BF16) for c in range(2)]
        piece = dot(chosen, jnp.concatenate(values, 0), ((1,), (1,)))
        total = piece if total is None else total + piece
    for s in range(box.slots):
        plane = total[s * ypad : (s + 1) * ypad]
        both = jnp.concatenate([plane, quarter(plane, zpad)], 0).astype(BF16)
        lines = dot(up_y_ref[...], both)
        for q in range(box.blocks):
            space_ref[q, s * slab : (s + 1) * slab, :] = lines[q * slab : (q + 1) * slab]
    used = box.slots * slab
    for q in range(box.blocks):
        if used < box.rows:
            space_ref[q, used:, :] = jnp.zeros((box.rows - used, space_ref.shape[2]), F32)
        out_ref[q] = space_ref[q].astype(BF16)


def folded_square(coord, grid):
    folded = jnp.where(coord >= grid // 2, coord - grid, coord)
    return folded * folded


def first_kernel(box, map_ref, value_ref, up_y_ref, out_ref, row_ref, z_ref, kinetic_ref, space_ref):
    grid, cell = box.grid, map_ref[...][None, :].astype(F32)
    local_x = jnp.floor((cell + 0.5) * (1.0 / (grid * grid)))
    cell = cell - local_x * (grid * grid)
    grid_y = jnp.floor((cell + 0.5) * (1.0 / grid))
    grid_z = cell - grid_y * grid
    grid_x = lax.axis_index("pw").astype(F32) + box.blocks * local_x
    squares = folded_square(grid_x, grid) + folded_square(grid_y, grid) + folded_square(grid_z, grid)
    kinetic_ref[...] = 1.5 * squares / float(grid // 2 * (grid // 2))

    def boxed(coord):
        moved = coord + box.half
        return jnp.where(moved >= grid, moved - grid, moved)

    slot = jnp.where(local_x < box.low, local_x, local_x - (box.slab - box.slots))
    row_ref[...] = (slot * box.ypad + boxed(grid_y)).astype(I32)
    z_ref[...] = boxed(grid_z).astype(I32)
    scattered(box, row_ref, z_ref, value_ref, up_y_ref, out_ref, space_ref)


def spread_rows(box, in_ref, from_ref):
    stride = box.spad * box.slab
    for p in range(box.blocks):
        for t in range(2 * box.zpad // 128):
            from_ref[t, p * stride : p * stride + box.rows, :] = in_ref[
                p, :, t * 128 : (t + 1) * 128
            ].astype(F32)
            if box.rows < stride:
                from_ref[t, p * stride + box.rows : (p + 1) * stride, :] = jnp.zeros(
                    (stride - box.rows, 128), F32
                )


def along_x(box, from_ref, up_x_ref, wide_ref):
    zpad, planes = box.zpad, box.blocks * box.spad
    both = []
    for line in range(box.slab):
        plane = jnp.concatenate(
            [from_ref[t, pl.ds(line, planes, stride=box.slab), :] for t in range(2 * zpad // 128)], 1
        )
        both.append(jnp.concatenate([plane, quarter(plane, zpad)], 0).astype(BF16))
    wide = dot(up_x_ref[...], jnp.concatenate(both, 1)).astype(BF16)
    for line in range(box.slab):
        wide_ref[line] = wide[:, line * 2 * zpad : (line + 1) * 2 * zpad]


def line_groups(box):
    return [slice(start, start + size) for start, size in chunks(box.slab, 5)]


def response_kernel(
    box,
    in_ref,
    pot_ref,
    up_x_ref,
    up_z_ref,
    real_ref,
    imag_ref,
    from_ref,
    wide_ref,
    pot_held,
    real_held,
    imag_held,
    sems,
    out_sems,
):
    copies = {
        lines.start: pltpu.make_async_copy(pot_ref.at[lines], pot_held.at[lines], sems.at[n])
        for n, lines in enumerate(line_groups(box))
    }
    for copy in copies.values():
        copy.start()
    spread_rows(box, in_ref, from_ref)
    along_x(box, from_ref, up_x_ref, wide_ref)
    outs = []
    for n, lines in enumerate(line_groups(box)):
        copies[lines.start].wait()
        for line in range(lines.start, lines.stop):
            for d, held in enumerate((real_held, imag_held)):
                held[line] = (pot_held[line] * dot(wide_ref[line], up_z_ref[d])).astype(BF16)
        for d, (held, ref) in enumerate(((real_held, real_ref), (imag_held, imag_ref))):
            outs.append(pltpu.make_async_copy(held.at[lines], ref.at[lines], out_sems.at[n, d]))
            outs[-1].start()
    for copy in outs:
        copy.wait()


def mix_kernel(
    box,
    in_ref,
    real_ref,
    imag_ref,
    con_ref,
    up_x_ref,
    down_x_ref,
    up_z_ref,
    down_z_ref,
    out_ref,
    from_ref,
    to_ref,
    wide_ref,
    back_ref,
    real_held,
    imag_held,
    con_held,
    sems,
):
    zpad, stride = box.zpad, box.spad * box.slab
    planes, tiles = box.blocks * box.spad, 2 * zpad // 128
    pairs = ((real_ref, real_held), (imag_ref, imag_held), (con_ref, con_held))
    copies = [
        [
            pltpu.make_async_copy(ref.at[lines], held.at[lines], sems.at[n, k])
            for k, (ref, held) in enumerate(pairs)
        ]
        for n, lines in enumerate(line_groups(box))
    ]
    for copy in sum(copies[:2], []):
        copy.start()
    spread_rows(box, in_ref, from_ref)
    along_x(box, from_ref, up_x_ref, wide_ref)
    for n, lines in enumerate(line_groups(box)):
        for copy in copies[n]:
            copy.wait()
        for copy in sum(copies[n + 2 : n + 3], []):
            copy.start()
        for line in range(lines.start, lines.stop):
            contact = con_held[line].astype(F32)
            mixed = [
                (held[line].astype(F32) + contact * dot(wide_ref[line], up_z_ref[d])).astype(BF16)
                for d, held in enumerate((real_held, imag_held))
            ]
            back = dot(mixed[0], down_z_ref[0]) + dot(mixed[1], down_z_ref[1])
            back_ref[:, line * 2 * zpad : (line + 1) * 2 * zpad] = back.astype(BF16)
    parts = dot(down_x_ref[...], back_ref[...])
    lined = parts[:planes] + quarter(parts[planes:], zpad)
    for line in range(box.slab):
        for t in range(tiles):
            column = (line * tiles + t) * 128
            to_ref[t, pl.ds(line, planes, stride=box.slab), :] = lined[:, column : column + 128]
    for p in range(box.blocks):
        for t in range(tiles):
            out_ref[p, :, t * 128 : (t + 1) * 128] = to_ref[
                t, p * stride : p * stride + box.rows, :
            ].astype(BF16)


def gather_kernel(mine_ref, other_ref, out_ref, sems):
    rows = mine_ref.shape[0]
    copies = [
        pltpu.make_async_copy(ref, out_ref.at[n * rows : (n + 1) * rows], sems.at[n])
        for n, ref in enumerate((mine_ref, other_ref))
    ]
    for copy in copies:
        copy.start()
    for copy in copies:
        copy.wait()


def term_kernel(
    box, in_ref, row_ref, z_ref, resp_ref, factor_ref, down_y_ref, low_ref, term_ref, space_ref
):
    zpad, ypad, slab = box.zpad, box.ypad, box.slab
    for q in range(box.blocks):
        space_ref[q] = in_ref[q].astype(F32)
    fields = []
    for s in range(box.slots):
        plane = jnp.concatenate(
            [space_ref[q, s * slab : (s + 1) * slab, :] for q in range(box.blocks)], 0
        ).astype(BF16)
        parts = dot(down_y_ref[...], plane)
        fields.append(parts[:ypad] + quarter(parts[ypad:], zpad))
    field = jnp.concatenate(fields, 0).T.astype(BF16)
    for start, size in chunks(box.count, 1024):
        span = slice(start, start + size)
        chosen = jnp.where(pick_rows(box.slots * ypad, row_ref[:, span]), 1.0, 0.0).astype(BF16)
        at_z = pick_rows(zpad, z_ref[:, span])
        found = dot(field, chosen)
        pair = resp_ref[0, :, span].astype(F32)
        rows = []
        for c in range(2):
            value = jnp.sum(jnp.where(at_z, found[c * zpad : (c + 1) * zpad], 0.0), 0, keepdims=True)
            own = (factor_ref[:, span] * pair[c : c + 1]).astype(BF16).astype(F32)
            rows.append(own + value)
        both = jnp.concatenate(rows, 0)
        term_ref[0, :, span] = both
        low_ref[0, :, span] = both.astype(BF16)


def call(kernel, out_shape, scratch, args, flops, limit, left=(), out_left=False):
    return pl.pallas_call(
        kernel,
        out_shape=out_shape,
        in_specs=[
            pl.BlockSpec(memory_space=pltpu.HBM if n in left else None) for n in range(len(args))
        ],
        out_specs=jax.tree.map(
            lambda _: pl.BlockSpec(memory_space=pltpu.HBM if out_left else None), out_shape
        ),
        scratch_shapes=scratch,
        compiler_params=pltpu.CompilerParams(vmem_limit_bytes=limit << 20),
        cost_estimate=pl.CostEstimate(flops=flops, bytes_accessed=4 << 20, transcendentals=0),
    )(*args)


def xor_permute(value, axis, size, distance):
    return lax.ppermute(value, axis, [(source, source ^ distance) for source in range(size)])


def sum_over(value, axis, size):
    near = 1
    while near < size:
        radix = 2 if (size // near).bit_length() % 2 == 0 else 4
        if radix == 2:
            value = value + xor_permute(value, axis, size, near)
        else:
            one, two, three = [xor_permute(value, axis, size, near * k) for k in (1, 2, 3)]
            value = (value + one) + (two + three)
        near *= radix
    return value


def on_device(sizes, response, panel, energies, offset, grid_map, potential, contact):
    rows_here, count = panel.shape[0], grid_map.shape[0]
    grid = potential.shape[0]
    bands, blocks = sizes
    box = Box(grid, blocks, count)
    up_y, down_y, up_x, down_x, up_z, down_z = box.tables()
    band_me = lax.axis_index("band")
    first_row = offset[0]

    shape = (blocks, box.rows, 2 * box.zpad)
    tiles, height = 2 * box.zpad // 128, blocks * box.spad * box.slab
    index_shape = jax.ShapeDtypeStruct((1, count), I32)
    field, row_index, z_index, kinetic = call(
        functools.partial(first_kernel, box),
        (
            jax.ShapeDtypeStruct(shape, BF16),
            index_shape,
            index_shape,
            jax.ShapeDtypeStruct((1, count), F32),
        ),
        [pltpu.VMEM(shape, F32)],
        (grid_map, response, up_y),
        1 << 31,
        56,
    )
    field, panel, contact = lax.optimization_barrier((field, panel, contact))
    contact_low = jnp.transpose(contact, (1, 0, 2)).astype(BF16)
    field = lax.all_to_all(field, "pw", split_axis=0, concat_axis=0, tiled=True)

    local = first_row - band_me * rows_here
    candidates = []
    for distance in range(bands):
        row = jnp.clip(local + (band_me ^ distance), 0, rows_here - 1)
        row = lax.dynamic_slice_in_dim(panel, row, 1, 0)
        candidates.append(xor_permute(row, "band", bands, distance) if distance else row)
    owner = (first_row + band_me) // rows_here
    partner = candidates[0]
    for distance in range(1, bands):
        partner = jnp.where(owner == band_me ^ distance, candidates[distance], partner)
    beside = with_layout_constraint(xor_permute(panel, "band", bands, 1), Layout((0, 1, 2)))
    shift = lax.dynamic_slice_in_dim(energies, first_row + band_me, 1, 0)
    factor = kinetic - shift[0]

    other_field = call(
        functools.partial(scattered, box),
        jax.ShapeDtypeStruct(shape, BF16),
        [pltpu.VMEM(shape, F32)],
        (row_index, z_index, partner, up_y),
        1 << 31,
        16,
    )
    other_field = lax.all_to_all(other_field, "pw", split_axis=0, concat_axis=0, tiled=True)
    groups = len(line_groups(box))
    space = (box.slab, grid, grid)
    columns = pltpu.VMEM((tiles, height, 128), F32)
    wide = pltpu.VMEM((box.slab, grid, 2 * box.zpad), BF16)
    real, imag = call(
        functools.partial(response_kernel, box),
        (jax.ShapeDtypeStruct(space, BF16), jax.ShapeDtypeStruct(space, BF16)),
        [
            columns,
            wide,
            pltpu.VMEM(space, F32),
            pltpu.VMEM(space, BF16),
            pltpu.VMEM(space, BF16),
            pltpu.SemaphoreType.DMA((groups,)),
            pltpu.SemaphoreType.DMA((groups, 2)),
        ],
        (field, jnp.transpose(potential, (1, 0, 2)), up_x, up_z),
        1 << 32,
        60,
        (1,),
        True,
    )
    returned = call(
        functools.partial(mix_kernel, box),
        jax.ShapeDtypeStruct(shape, BF16),
        [
            columns,
            columns,
            wide,
            pltpu.VMEM((grid, box.slab * 2 * box.zpad), BF16),
            pltpu.VMEM(space, BF16),
            pltpu.VMEM(space, BF16),
            pltpu.VMEM(space, BF16),
            pltpu.SemaphoreType.DMA((groups, 3)),
        ],
        (other_field, real, imag, contact_low, up_x, down_x, up_z, down_z),
        1 << 32,
        60,
        (1, 2, 3),
    )
    returned, panel_late, beside = lax.optimization_barrier((returned, panel, beside))
    rows_both = pl.pallas_call(
        gather_kernel,
        out_shape=jax.ShapeDtypeStruct((2 * rows_here, 2, count), BF16),
        in_specs=[pl.BlockSpec(memory_space=pl.ANY)] * 2,
        out_specs=pl.BlockSpec(memory_space=pltpu.VMEM),
        scratch_shapes=[pltpu.SemaphoreType.DMA((2,))],
        compiler_params=pltpu.CompilerParams(vmem_limit_bytes=16 << 20),
        cost_estimate=pl.CostEstimate(flops=0, bytes_accessed=8 << 20, transcendentals=0),
    )(panel_late, beside)
    combed = lax.all_to_all(returned, "pw", split_axis=0, concat_axis=0, tiled=True)
    combed, rows_both = lax.optimization_barrier((combed, rows_both))
    term_low, term = call(
        functools.partial(term_kernel, box),
        (
            jax.ShapeDtypeStruct((1, 2, count), BF16),
            jax.ShapeDtypeStruct((1, 2, count), F32),
        ),
        [pltpu.VMEM(shape, F32)],
        (combed, row_index, z_index, response, factor, down_y),
        1 << 32,
        16,
    )

    far = range(2, bands, 2)
    terms = jnp.concatenate(
        [term_low] + [xor_permute(term_low, "band", bands, k) for k in far], 0
    )
    other = jnp.stack([terms[:, 1], -terms[:, 0]], axis=1)
    swapped = jnp.stack([terms, other])
    correlation = jnp.einsum("mcj,dncj->dmn", rows_both, swapped, preferred_element_type=F32)
    low = sum_over(correlation, "pw", blocks).astype(BF16)
    spread = jnp.stack([jnp.stack([low[0], -low[1]]), jnp.stack([low[1], low[0]])])
    shares = jnp.einsum("mcj,dcmn->ndj", rows_both, spread, preferred_element_type=F32)
    correction = shares[:1]
    for k, distance in enumerate(far):
        share = xor_permute(shares[k + 1 : k + 2].astype(BF16), "band", bands, distance)
        correction = correction + share.astype(F32)
    summed = term - correction
    residual = summed.astype(BF16)
    response_next = (response.astype(F32) - summed / (1.0 + kinetic)[None]).astype(BF16)
    return (residual, response_next)


def solution(mesh):
    return jax.shard_map(
        functools.partial(on_device, (mesh.shape["band"], mesh.shape["pw"])),
        mesh=mesh,
        in_specs=(
            P("band", None, "pw"),
            P("band", None, "pw"),
            P(),
            P(),
            P("pw"),
            P(None, "pw", None),
            P(None, "pw", None),
        ),
        out_specs=(P("band", None, "pw"), P("band", None, "pw")),
        check_vma=False,
    )
```

```python
import functools
import math

import jax
import jax.numpy as jnp
import numpy as np
from jax import lax
from jax.experimental import pallas as pl
from jax.experimental.layout import Layout, with_layout_constraint
from jax.experimental.pallas import tpu as pltpu
from jax.sharding import PartitionSpec as P

F32, BF16, I32 = jnp.float32, jnp.bfloat16, jnp.int32


SCATTER_LIMIT, MIX_LIMIT = 24, 16


def up(value, step):
    return -(-value // step) * step


class Box:
    def __init__(self, grid, blocks, count):
        self.grid, self.blocks, self.count = grid, blocks, count
        self.slab = grid // blocks
        folded = np.arange(grid)
        folded = np.where(folded >= grid // 2, folded - grid, folded)
        flat = np.sort((folded[:, None] ** 2 + folded[None, :] ** 2).ravel())
        used, half = set(), 0
        for block in range(blocks):
            planes = folded[block + blocks * np.arange(self.slab)] ** 2
            radii = np.sort((planes[:, None] + flat[None, :]).ravel())
            limit = int(radii[count - 1])
            used |= set(np.nonzero(planes <= limit)[0].tolist())
            half = max(half, math.isqrt(limit - int(planes.min())))
        self.low = 0
        while self.low in used and self.low < self.slab:
            self.low += 1
        self.slots = self.low + len([u for u in used if u >= self.low])
        if any(u in used for u in range(self.low, self.slab - (self.slots - self.low))):
            self.low = self.slots = self.slab
        self.planes = [s if s < self.low else s + self.slab - self.slots for s in range(self.slots)]
        self.half = min(half, grid // 2 - 1) if 2 * half + 1 <= grid else grid // 2
        self.width = min(2 * self.half + 1, grid)
        self.ypad = up(self.width, 8)
        self.zpad = 64 if self.width <= 64 else up(self.width, 128)
        self.rows = up(self.slots * self.slab, 16)
        self.spad = self.slots
        while self.spad * self.slab % 8 or self.spad * self.slab < self.rows:
            self.spad += 1

    def waves(self, first, other):
        products = (np.asarray(first)[:, None] * np.asarray(other)[None, :]) % self.grid
        angles = products.astype(np.float32) * np.float32(2.0 * math.pi / self.grid)
        scaling = np.float32(1.0 / math.sqrt(self.grid))
        return np.cos(angles) * scaling, np.sin(angles) * scaling

    def tables(self):
        grid, ypad, zpad = self.grid, self.ypad, self.zpad
        every = np.arange(grid)
        boxed = np.arange(self.width) - self.half

        def padded(part, rows, columns):
            return np.pad(part, ((0, rows - part.shape[0]), (0, columns - part.shape[1])))

        cos_y, sin_y = self.waves(every, boxed)
        up_y = np.concatenate([padded(cos_y, grid, ypad), padded(sin_y, grid, ypad)], 1)
        down_y = np.concatenate([padded(cos_y.T, ypad, grid), padded(-sin_y.T, ypad, grid)], 0)
        cos_z, sin_z = padded(cos_y, grid, zpad), padded(sin_y, grid, zpad)
        cos_z, sin_z = (padded(part, up(grid, 128), zpad) for part in (cos_z, sin_z))
        up_z = np.stack([np.concatenate([cos_z.T, -sin_z.T], 0), np.concatenate([sin_z.T, cos_z.T], 0)])
        down_z = np.concatenate(
            [np.concatenate([cos_z, -sin_z], 1), np.concatenate([sin_z, cos_z], 1)], 0
        )
        planes = np.array([p + self.blocks * x for p in range(self.blocks) for x in self.planes])
        cos_x, sin_x = self.waves(every, planes)

        def slotted(part):
            part = part.reshape(grid, self.blocks, self.slots)
            part = np.pad(part, ((0, 0), (0, 0), (0, self.spad - self.slots)))
            return part.reshape(grid, self.blocks * self.spad)

        cos_x, sin_x = slotted(cos_x), slotted(sin_x)
        up_x = np.concatenate([cos_x, sin_x], 1)
        down_x = np.concatenate([cos_x.T, -sin_x.T], 0)
        return [jnp.asarray(t, BF16) for t in (up_y, down_y, up_x, down_x, up_z, down_z)]


def quarter(field, zpad):
    pieces = []
    for start in range(0, field.shape[1], 2 * zpad):
        piece = field[:, start : start + 2 * zpad]
        if 2 * zpad == 128:
            lane = lax.broadcasted_iota(I32, piece.shape, 1)
            turned = pltpu.roll(piece, zpad, 1)
            pieces.append(jnp.where(lane < zpad, -turned, turned))
        else:
            pieces += [-piece[:, zpad:], piece[:, :zpad]]
    return pieces[0] if len(pieces) == 1 else jnp.concatenate(pieces, 1)


def chunks(total, step):
    return [(start, min(step, total - start)) for start in range(0, total, step)]


def dot(left, right, dims=((1,), (0,))):
    return lax.dot_general(left, right, (dims, ((), ())), preferred_element_type=F32)


def pick_rows(rows, index):
    return lax.broadcasted_iota(I32, (rows, index.shape[1]), 0) == index


def scatter_kernel(box, choice_ref, row_ref, z_ref, resp_ref, *refs):
    *partner_refs, up_y_ref, out_ref, space_ref = refs
    zpad, ypad, slab = box.zpad, box.ypad, box.slab
    choice, total = choice_ref[0], None
    for start, size in chunks(box.count, 1024):
        span = slice(start, start + size)
        chosen = jnp.where(pick_rows(box.slots * ypad, row_ref[:, span]), 1.0, 0.0).astype(BF16)
        at_z = pick_rows(zpad, z_ref[:, span])
        partner = partner_refs[0][0, :, span].astype(F32)
        for k, ref in enumerate(partner_refs[1:]):
            partner = jnp.where(choice == k + 1, ref[0, :, span].astype(F32), partner)
        values = [
            jnp.where(at_z, pair[c : c + 1], 0.0).astype(BF16)
            for pair in (resp_ref[0, :, span].astype(F32), partner)
            for c in range(2)
        ]
        piece = dot(chosen, jnp.concatenate(values, 0), ((1,), (1,)))
        total = piece if total is None else total + piece
    for s in range(box.slots):
        plane = total[s * ypad : (s + 1) * ypad]
        both = jnp.concatenate([plane, quarter(plane, zpad)], 0).astype(BF16)
        lines = dot(up_y_ref[...], both)
        for q in range(box.blocks):
            space_ref[q, s * slab : (s + 1) * slab, :] = lines[q * slab : (q + 1) * slab]
    used = box.slots * slab
    for q in range(box.blocks):
        if used < box.rows:
            space_ref[q, used:, :] = jnp.zeros((box.rows - used, space_ref.shape[2]), F32)
        out_ref[q] = space_ref[q].astype(BF16)


def folded_square(coord, grid):
    folded = jnp.where(coord >= grid // 2, coord - grid, coord)
    return folded * folded


def index_kernel(box, map_ref, resp_ref, table_ref, row_ref, z_ref, kinetic_ref, resp_out, table_out):
    grid, cell = box.grid, map_ref[...][None, :].astype(F32)
    local_x = jnp.floor((cell + 0.5) * (1.0 / (grid * grid)))
    cell = cell - local_x * (grid * grid)
    grid_y = jnp.floor((cell + 0.5) * (1.0 / grid))
    grid_z = cell - grid_y * grid
    grid_x = lax.axis_index("pw").astype(F32) + box.blocks * local_x
    squares = folded_square(grid_x, grid) + folded_square(grid_y, grid) + folded_square(grid_z, grid)
    kinetic_ref[...] = 1.5 * squares / float(grid // 2 * (grid // 2))

    def boxed(coord):
        moved = coord + box.half
        return jnp.where(moved >= grid, moved - grid, moved)

    slot = jnp.where(local_x < box.low, local_x, local_x - (box.slab - box.slots))
    row_ref[...] = (slot * box.ypad + boxed(grid_y)).astype(I32)
    z_ref[...] = boxed(grid_z).astype(I32)
    resp_out[...] = resp_ref[...]
    table_out[...] = table_ref[...]


def spread_rows(box, in_ref, from_ref):
    stride = box.spad * box.slab
    for p in range(box.blocks):
        for t in range(from_ref.shape[0]):
            from_ref[t, p * stride : p * stride + box.rows, :] = in_ref[
                p, :, t * 128 : (t + 1) * 128
            ].astype(F32)
            if box.rows < stride:
                from_ref[t, p * stride + box.rows : (p + 1) * stride, :] = jnp.zeros(
                    (stride - box.rows, 128), F32
                )


def along_x(box, from_ref, field, up_x_ref, wide_ref):
    zpad, planes = box.zpad, box.blocks * box.spad
    tiles = 2 * zpad // 128
    both = []
    for line in range(box.slab):
        plane = jnp.concatenate(
            [
                from_ref[field * tiles + t, pl.ds(line, planes, stride=box.slab), :]
                for t in range(tiles)
            ],
            1,
        )
        both.append(jnp.concatenate([plane, quarter(plane, zpad)], 0).astype(BF16))
    wide = dot(up_x_ref[...], jnp.concatenate(both, 1)).astype(BF16)
    for line in range(box.slab):
        wide_ref[field, line] = wide[:, line * 2 * zpad : (line + 1) * 2 * zpad]


def x_kernel(box, in_ref, up_x_ref, wide_ref, from_ref):
    spread_rows(box, in_ref, from_ref)
    for field in range(2):
        along_x(box, from_ref, field, up_x_ref, wide_ref)


def mix_kernel(
    box, wide_ref, pot_ref, con_ref, down_x_ref, up_z_ref, down_z_ref, out_ref, to_ref, back_ref
):
    zpad, stride = box.zpad, box.spad * box.slab
    planes, tiles = box.blocks * box.spad, 2 * zpad // 128
    pair = 2 if box.slab % 2 == 0 else 1
    for first in range(0, box.slab, pair):
        lines = range(first, first + pair)
        potential, contact, resp, part = (
            jnp.concatenate([ref[line] for line in lines], 0)
            for ref in (pot_ref, con_ref, wide_ref.at[0], wide_ref.at[1])
        )
        potential, contact = potential.astype(F32), contact.astype(F32)
        mixed = [
            (potential * dot(resp, up_z_ref[d]) + contact * dot(part, up_z_ref[d])).astype(BF16)
            for d in range(2)
        ]
        back = dot(jnp.concatenate(mixed, 1), down_z_ref[...]).astype(BF16)
        for n, line in enumerate(lines):
            back_ref[:, line * 2 * zpad : (line + 1) * 2 * zpad] = back[
                n * box.grid : (n + 1) * box.grid
            ]
    parts = dot(down_x_ref[...], back_ref[...])
    lined = parts[:planes] + quarter(parts[planes:], zpad)
    for line in range(box.slab):
        for t in range(tiles):
            column = (line * tiles + t) * 128
            to_ref[t, pl.ds(line, planes, stride=box.slab), :] = lined[:, column : column + 128]
    for p in range(box.blocks):
        for t in range(tiles):
            out_ref[p, :, t * 128 : (t + 1) * 128] = to_ref[
                t, p * stride : p * stride + box.rows, :
            ].astype(BF16)


def gather_kernel(mine_ref, other_ref, out_ref, sems):
    rows = mine_ref.shape[0]
    copies = [
        pltpu.make_async_copy(ref, out_ref.at[n * rows : (n + 1) * rows], sems.at[n])
        for n, ref in enumerate((mine_ref, other_ref))
    ]
    for copy in copies:
        copy.start()
    for copy in copies:
        copy.wait()


def term_kernel(
    box, in_ref, row_ref, z_ref, resp_ref, factor_ref, down_y_ref, low_ref, term_ref, space_ref
):
    zpad, ypad, slab = box.zpad, box.ypad, box.slab
    for q in range(box.blocks):
        space_ref[q] = in_ref[q].astype(F32)
    fields = []
    for s in range(box.slots):
        plane = jnp.concatenate(
            [space_ref[q, s * slab : (s + 1) * slab, :] for q in range(box.blocks)], 0
        ).astype(BF16)
        parts = dot(down_y_ref[...], plane)
        fields.append(parts[:ypad] + quarter(parts[ypad:], zpad))
    field = jnp.concatenate(fields, 0).T.astype(BF16)
    for start, size in chunks(box.count, 1024):
        span = slice(start, start + size)
        chosen = jnp.where(pick_rows(box.slots * ypad, row_ref[:, span]), 1.0, 0.0).astype(BF16)
        at_z = pick_rows(zpad, z_ref[:, span])
        found = dot(field, chosen)
        pair = resp_ref[0, :, span].astype(F32)
        rows = []
        for c in range(2):
            value = jnp.sum(jnp.where(at_z, found[c * zpad : (c + 1) * zpad], 0.0), 0, keepdims=True)
            own = (factor_ref[:, span] * pair[c : c + 1]).astype(BF16).astype(F32)
            rows.append(own + value)
        both = jnp.concatenate(rows, 0)
        term_ref[0, :, span] = both
        low_ref[0, :, span] = both.astype(BF16)


def call(kernel, out_shape, scratch, args, flops, limit, left=(), resident=(), scalars=()):
    def space(n):
        if n in left:
            return pltpu.HBM
        return pltpu.VMEM if n in resident else pltpu.SMEM if n in scalars else None

    return pl.pallas_call(
        kernel,
        out_shape=out_shape,
        in_specs=[pl.BlockSpec(memory_space=space(n)) for n in range(len(args))],
        scratch_shapes=scratch,
        compiler_params=pltpu.CompilerParams(vmem_limit_bytes=limit << 20),
        cost_estimate=pl.CostEstimate(flops=flops, bytes_accessed=4 << 20, transcendentals=0),
    )(*args)


def xor_permute(value, axis, size, distance):
    return lax.ppermute(value, axis, [(source, source ^ distance) for source in range(size)])


def sum_over(value, axis, size):
    near = 1
    while near < size:
        radix = 2 if (size // near).bit_length() % 2 == 0 else 4
        if radix == 2:
            value = value + xor_permute(value, axis, size, near)
        else:
            one, two, three = [xor_permute(value, axis, size, near * k) for k in (1, 2, 3)]
            value = (value + one) + (two + three)
        near *= radix
    return value


def on_device(sizes, response, panel, energies, offset, grid_map, potential, contact):
    rows_here, count = panel.shape[0], grid_map.shape[0]
    grid = potential.shape[0]
    bands, blocks = sizes
    box = Box(grid, blocks, count)
    up_y, down_y, up_x, down_x, up_z, down_z = box.tables()
    band_me = lax.axis_index("band")
    first_row = offset[0]

    local = first_row - band_me * rows_here
    candidates = []
    for distance in range(bands):
        row = jnp.clip(local + (band_me ^ distance), 0, rows_here - 1)
        row = lax.dynamic_slice_in_dim(panel, row, 1, 0)
        candidates.append(xor_permute(row, "band", bands, distance) if distance else row)
    owner = (first_row + band_me) // rows_here
    choice = (owner ^ band_me)[None]

    index_shape = jax.ShapeDtypeStruct((1, count), I32)
    row_index, z_index, kinetic, resp_here, up_y_here = call(
        functools.partial(index_kernel, box),
        (
            index_shape,
            index_shape,
            jax.ShapeDtypeStruct((1, count), F32),
            jax.ShapeDtypeStruct(response.shape, BF16),
            jax.ShapeDtypeStruct(up_y.shape, BF16),
        ),
        [],
        (grid_map, response, up_y),
        1 << 20,
        16,
    )
    shape = (blocks, box.rows, 2 * box.zpad)
    both_shape = (blocks, box.rows, 4 * box.zpad)
    field = call(
        functools.partial(scatter_kernel, box),
        jax.ShapeDtypeStruct(both_shape, BF16),
        [pltpu.VMEM(both_shape, F32)],
        (choice, row_index, z_index, resp_here, *candidates, up_y_here),
        1 << 32,
        SCATTER_LIMIT,
        (),
        range(1, 5 + bands),
        (0,),
    )
    field, panel_sent, potential, contact = lax.optimization_barrier((field, panel, potential, contact))
    potential_low, contact_low = (
        jnp.pad(jnp.transpose(value, (1, 0, 2)).astype(BF16), ((0, 0), (0, 0), (0, -grid % 128)))
        for value in (potential, contact)
    )
    beside = with_layout_constraint(xor_permute(panel_sent, "band", bands, 1), Layout((0, 1, 2)))
    shift = lax.dynamic_slice_in_dim(energies, first_row + band_me, 1, 0)
    factor = kinetic - shift[0]
    field = lax.all_to_all(field, "pw", split_axis=0, concat_axis=0, tiled=True)

    tiles, height = 2 * box.zpad // 128, blocks * box.spad * box.slab
    wide = call(
        functools.partial(x_kernel, box),
        jax.ShapeDtypeStruct((2, box.slab, grid, 2 * box.zpad), BF16),
        [pltpu.VMEM((2 * tiles, height, 128), F32)],
        (field, up_x),
        1 << 31,
        MIX_LIMIT,
        (),
        range(2),
    )
    returned = call(
        functools.partial(mix_kernel, box),
        jax.ShapeDtypeStruct(shape, BF16),
        [
            pltpu.VMEM((tiles, height, 128), F32),
            pltpu.VMEM((grid, box.slab * 2 * box.zpad), BF16),
        ],
        (wide, potential_low, contact_low, down_x, up_z, down_z),
        1 << 32,
        MIX_LIMIT,
        (),
        range(6),
    )
    returned, panel_late, beside = lax.optimization_barrier((returned, panel, beside))
    rows_both = pl.pallas_call(
        gather_kernel,
        out_shape=jax.ShapeDtypeStruct((2 * rows_here, 2, count), BF16),
        in_specs=[pl.BlockSpec(memory_space=pl.ANY)] * 2,
        out_specs=pl.BlockSpec(memory_space=pltpu.VMEM),
        scratch_shapes=[pltpu.SemaphoreType.DMA((2,))],
        compiler_params=pltpu.CompilerParams(vmem_limit_bytes=16 << 20),
        cost_estimate=pl.CostEstimate(flops=0, bytes_accessed=8 << 20, transcendentals=0),
    )(panel_late, beside)
    combed = lax.all_to_all(returned, "pw", split_axis=0, concat_axis=0, tiled=True)
    combed, rows_both = lax.optimization_barrier((combed, rows_both))
    term_low, term = call(
        functools.partial(term_kernel, box),
        (
            jax.ShapeDtypeStruct((1, 2, count), BF16),
            jax.ShapeDtypeStruct((1, 2, count), F32),
        ),
        [pltpu.VMEM(shape, F32)],
        (combed, row_index, z_index, response, factor, down_y),
        1 << 32,
        16,
    )

    far = range(2, bands, 2)
    terms = jnp.concatenate(
        [term_low] + [xor_permute(term_low, "band", bands, k) for k in far], 0
    )
    other = jnp.stack([terms[:, 1], -terms[:, 0]], axis=1)
    swapped = jnp.stack([terms, other])
    correlation = jnp.einsum("mcj,dncj->dmn", rows_both, swapped, preferred_element_type=F32)
    low = sum_over(correlation, "pw", blocks).astype(BF16)
    spread = jnp.stack([jnp.stack([low[0], -low[1]]), jnp.stack([low[1], low[0]])])
    shares = jnp.einsum("mcj,dcmn->ndj", rows_both, spread, preferred_element_type=F32)
    correction = shares[:1]
    for k, distance in enumerate(far):
        share = xor_permute(shares[k + 1 : k + 2].astype(BF16), "band", bands, distance)
        correction = correction + share.astype(F32)
    summed = term - correction
    residual = summed.astype(BF16)
    response_next = (response.astype(F32) - summed / (1.0 + kinetic)[None]).astype(BF16)
    return (residual, response_next)


def solution(mesh):
    return jax.shard_map(
        functools.partial(on_device, (mesh.shape["band"], mesh.shape["pw"])),
        mesh=mesh,
        in_specs=(
            P("band", None, "pw"),
            P("band", None, "pw"),
            P(),
            P(),
            P("pw"),
            P(None, "pw", None),
            P(None, "pw", None),
        ),
        out_specs=(P("band", None, "pw"), P("band", None, "pw")),
        check_vma=False,
    )
```

```python
import functools
import math

import jax
import jax.numpy as jnp
import numpy as np
from jax import lax
from jax.experimental import pallas as pl
from jax.experimental.layout import Layout, with_layout_constraint
from jax.experimental.pallas import tpu as pltpu
from jax.sharding import PartitionSpec as P

F32, BF16, I32 = jnp.float32, jnp.bfloat16, jnp.int32


SCATTER_LIMIT, MIX_LIMIT = 24, 16


def up(value, step):
    return -(-value // step) * step


class Box:
    def __init__(self, grid, blocks, count):
        self.grid, self.blocks, self.count = grid, blocks, count
        self.slab = grid // blocks
        folded = np.arange(grid)
        folded = np.where(folded >= grid // 2, folded - grid, folded)
        flat = np.sort((folded[:, None] ** 2 + folded[None, :] ** 2).ravel())
        used, half, limits = set(), 0, []
        for block in range(blocks):
            planes = folded[block + blocks * np.arange(self.slab)] ** 2
            radii = np.sort((planes[:, None] + flat[None, :]).ravel())
            limit = int(radii[count - 1])
            limits.append(limit)
            used |= set(np.nonzero(planes <= limit)[0].tolist())
            half = max(half, math.isqrt(limit - int(planes.min())))
        self.low = 0
        while self.low in used and self.low < self.slab:
            self.low += 1
        self.slots = self.low + len([u for u in used if u >= self.low])
        if any(u in used for u in range(self.low, self.slab - (self.slots - self.low))):
            self.low = self.slots = self.slab
        self.planes = [s if s < self.low else s + self.slab - self.slots for s in range(self.slots)]
        self.half = min(half, grid // 2 - 1) if 2 * half + 1 <= grid else grid // 2
        self.width = min(2 * self.half + 1, grid)
        self.ypad = up(self.width, 8)
        self.zpad = 64 if self.width <= 64 else up(self.width, 128)
        reach = []
        for x in self.planes:
            held = [
                math.isqrt(limit - int(folded[block + blocks * x]) ** 2)
                for block, limit in enumerate(limits)
                if int(folded[block + blocks * x]) ** 2 <= limit
            ]
            reach.append(max(held, default=0))
        narrow = int(np.argmin(reach))
        fits = self.slots > 1 and 2 * reach[narrow] + 1 <= self.zpad - self.width
        self.order = [s for s in range(self.slots) if s != narrow] + [narrow]
        self.narrow, self.reach = (narrow if fits else None), reach[narrow]
        self.turn = self.width - self.half + self.reach
        self.sent = self.slots - 1 if fits else self.slots
        self.rows = up(self.sent * self.slab, 16)
        self.spad = self.slots
        while self.spad * self.slab % 8 or self.spad * self.slab < self.rows:
            self.spad += 1

    def waves(self, first, other):
        products = (np.asarray(first)[:, None] * np.asarray(other)[None, :]) % self.grid
        angles = products.astype(np.float32) * np.float32(2.0 * math.pi / self.grid)
        scaling = np.float32(1.0 / math.sqrt(self.grid))
        return np.cos(angles) * scaling, np.sin(angles) * scaling

    def tables(self):
        grid, ypad, zpad = self.grid, self.ypad, self.zpad
        every = np.arange(grid)
        boxed = np.arange(self.width) - self.half

        def padded(part, rows, columns):
            return np.pad(part, ((0, rows - part.shape[0]), (0, columns - part.shape[1])))

        cos_y, sin_y = self.waves(every, boxed)
        down_y = np.concatenate([padded(cos_y.T, ypad, grid), padded(-sin_y.T, ypad, grid)], 0)
        cos_z, sin_z = padded(cos_y, grid, zpad), padded(sin_y, grid, zpad)
        cos_z, sin_z = (padded(part, up(grid, 128), zpad) for part in (cos_z, sin_z))
        up_z = np.stack([np.concatenate([cos_z.T, -sin_z.T], 0), np.concatenate([sin_z.T, cos_z.T], 0)])
        down_z = np.concatenate(
            [np.concatenate([cos_z, -sin_z], 1), np.concatenate([sin_z, cos_z], 1)], 0
        )
        planes = np.array([p + self.blocks * x for p in range(self.blocks) for x in (self.planes[s] for s in self.order)])
        cos_x, sin_x = self.waves(every, planes)

        def slotted(part):
            part = part.reshape(grid, self.blocks, self.slots)
            part = np.pad(part, ((0, 0), (0, 0), (0, self.spad - self.slots)))
            return part.reshape(grid, self.blocks * self.spad)

        cos_x, sin_x = slotted(cos_x), slotted(sin_x)
        up_x = np.concatenate([cos_x, sin_x], 1)
        down_x = np.concatenate([cos_x.T, -sin_x.T], 0)
        return [jnp.asarray(t, BF16) for t in (down_y, up_x, down_x, up_z, down_z)]


def quarter(field, zpad):
    pieces = []
    for start in range(0, field.shape[1], 2 * zpad):
        piece = field[:, start : start + 2 * zpad]
        if 2 * zpad == 128:
            lane = lax.broadcasted_iota(I32, piece.shape, 1)
            turned = pltpu.roll(piece, zpad, 1)
            pieces.append(jnp.where(lane < zpad, -turned, turned))
        else:
            pieces += [-piece[:, zpad:], piece[:, :zpad]]
    return pieces[0] if len(pieces) == 1 else jnp.concatenate(pieces, 1)


def moved(box, field, back):
    pieces, span = [], 2 * box.zpad
    least = box.half - box.reach if back else box.width
    for start in range(0, field.shape[1], span):
        piece = field[:, start : start + span]
        turned = pltpu.roll(piece, span - box.turn if back else box.turn, 1)
        lane = lax.broadcasted_iota(I32, piece.shape, 1)
        lane = jnp.where(lane >= box.zpad, lane - box.zpad, lane)
        inside = (lane >= least) & (lane <= least + 2 * box.reach)
        pieces.append(jnp.where(inside, turned, 0.0))
    return pieces[0] if len(pieces) == 1 else jnp.concatenate(pieces, 1)


def chunks(total, step):
    return [(start, min(step, total - start)) for start in range(0, total, step)]


def dot(left, right, dims=((1,), (0,))):
    return lax.dot_general(left, right, (dims, ((), ())), preferred_element_type=F32)


def pick_rows(rows, index):
    return lax.broadcasted_iota(I32, (rows, index.shape[1]), 0) == index


def scatter_kernel(box, choice_ref, row_ref, z_ref, resp_ref, *refs):
    *partner_refs, up_y_ref, out_ref, space_ref = refs
    zpad, ypad, slab = box.zpad, box.ypad, box.slab
    choice, total = choice_ref[0], None
    for start, size in chunks(box.count, 1024):
        span = slice(start, start + size)
        chosen = jnp.where(pick_rows(box.slots * ypad, row_ref[:, span]), 1.0, 0.0).astype(BF16)
        at_z = pick_rows(zpad, z_ref[:, span])
        partner = partner_refs[0][0, :, span].astype(F32)
        for k, ref in enumerate(partner_refs[1:]):
            partner = jnp.where(choice == k + 1, ref[0, :, span].astype(F32), partner)
        values = [
            jnp.where(at_z, pair[c : c + 1], 0.0).astype(BF16)
            for pair in (resp_ref[0, :, span].astype(F32), partner)
            for c in range(2)
        ]
        piece = dot(chosen, jnp.concatenate(values, 0), ((1,), (1,)))
        total = piece if total is None else total + piece
    added = None
    for n, s in reversed(list(enumerate(box.order))):
        plane = total[s * ypad : (s + 1) * ypad]
        both = jnp.concatenate([plane, quarter(plane, zpad)], 0).astype(BF16)
        lines = dot(up_y_ref[...], both)
        if n == box.sent:
            added = moved(box, lines, False)
            continue
        if n == 0 and added is not None:
            lines = lines + added
        for q in range(box.blocks):
            space_ref[q, n * slab : (n + 1) * slab, :] = lines[q * slab : (q + 1) * slab]
    used = box.sent * slab
    for q in range(box.blocks):
        if used < box.rows:
            space_ref[q, used:, :] = jnp.zeros((box.rows - used, space_ref.shape[2]), F32)
        out_ref[q] = space_ref[q].astype(BF16)


def folded_square(coord, grid):
    folded = jnp.where(coord >= grid // 2, coord - grid, coord)
    return folded * folded


def index_kernel(box, map_ref, resp_ref, row_ref, z_ref, kinetic_ref, resp_out, table_ref):
    grid, cell = box.grid, map_ref[...][None, :].astype(F32)
    local_x = jnp.floor((cell + 0.5) * (1.0 / (grid * grid)))
    cell = cell - local_x * (grid * grid)
    grid_y = jnp.floor((cell + 0.5) * (1.0 / grid))
    grid_z = cell - grid_y * grid
    grid_x = lax.axis_index("pw").astype(F32) + box.blocks * local_x
    squares = folded_square(grid_x, grid) + folded_square(grid_y, grid) + folded_square(grid_z, grid)
    kinetic_ref[...] = 1.5 * squares / float(grid // 2 * (grid // 2))

    def boxed(coord):
        moved = coord + box.half
        return jnp.where(moved >= grid, moved - grid, moved)

    slot = jnp.where(local_x < box.low, local_x, local_x - (box.slab - box.slots))
    row_ref[...] = (slot * box.ypad + boxed(grid_y)).astype(I32)
    z_ref[...] = boxed(grid_z).astype(I32)
    resp_out[...] = resp_ref[...]
    line = lax.broadcasted_iota(I32, table_ref.shape, 0).astype(F32)
    column = lax.broadcasted_iota(I32, table_ref.shape, 1)
    sine = column >= box.ypad
    column = jnp.where(sine, column - box.ypad, column)
    products = line * (column - box.half).astype(F32)
    products = products - jnp.floor((products + 0.5) * (1.0 / grid)) * grid
    products = jnp.where(sine, products - grid / 4, products)
    waves = jnp.cos(products * (2.0 * math.pi / grid)) * (1.0 / math.sqrt(grid))
    table_ref[...] = jnp.where(column < box.width, waves, 0.0).astype(BF16)


def spread_rows(box, in_ref, from_ref):
    stride = box.spad * box.slab
    for p in range(box.blocks):
        for t in range(from_ref.shape[0]):
            from_ref[t, p * stride : p * stride + box.rows, :] = in_ref[
                p, :, t * 128 : (t + 1) * 128
            ].astype(F32)
            if box.rows < stride:
                from_ref[t, p * stride + box.rows : (p + 1) * stride, :] = jnp.zeros(
                    (stride - box.rows, 128), F32
                )
        if box.narrow is None:
            continue
        first = p * stride + box.sent * box.slab
        neighbour = moved(box, in_ref[p].astype(F32)[: box.slab], True)
        for t in range(from_ref.shape[0]):
            from_ref[t, first : first + box.slab, :] = neighbour[:, t * 128 : (t + 1) * 128]


def along_x(box, from_ref, field, up_x_ref, wide_ref):
    zpad, planes = box.zpad, box.blocks * box.spad
    tiles = 2 * zpad // 128
    both = []
    for line in range(box.slab):
        plane = jnp.concatenate(
            [
                from_ref[field * tiles + t, pl.ds(line, planes, stride=box.slab), :]
                for t in range(tiles)
            ],
            1,
        )
        both.append(jnp.concatenate([plane, quarter(plane, zpad)], 0).astype(BF16))
    wide = dot(up_x_ref[...], jnp.concatenate(both, 1)).astype(BF16)
    for line in range(box.slab):
        wide_ref[field, line] = wide[:, line * 2 * zpad : (line + 1) * 2 * zpad]


def x_kernel(box, in_ref, up_x_ref, wide_ref, from_ref):
    spread_rows(box, in_ref, from_ref)
    for field in range(2):
        along_x(box, from_ref, field, up_x_ref, wide_ref)


def mix_kernel(
    box, wide_ref, pot_ref, con_ref, down_x_ref, up_z_ref, down_z_ref, out_ref, to_ref, back_ref
):
    zpad, stride = box.zpad, box.spad * box.slab
    planes, tiles = box.blocks * box.spad, 2 * zpad // 128
    pair = 2 if box.slab % 2 == 0 else 1
    for first in range(0, box.slab, pair):
        lines = range(first, first + pair)
        potential, contact, resp, part = (
            jnp.concatenate([ref[line] for line in lines], 0)
            for ref in (pot_ref, con_ref, wide_ref.at[0], wide_ref.at[1])
        )
        potential, contact = potential.astype(F32), contact.astype(F32)
        mixed = [
            (potential * dot(resp, up_z_ref[d]) + contact * dot(part, up_z_ref[d])).astype(BF16)
            for d in range(2)
        ]
        back = dot(jnp.concatenate(mixed, 1), down_z_ref[...]).astype(BF16)
        for n, line in enumerate(lines):
            back_ref[:, line * 2 * zpad : (line + 1) * 2 * zpad] = back[
                n * box.grid : (n + 1) * box.grid
            ]
    parts = dot(down_x_ref[...], back_ref[...])
    lined = parts[:planes] + quarter(parts[planes:], zpad)
    for line in range(box.slab):
        for t in range(tiles):
            column = (line * tiles + t) * 128
            to_ref[t, pl.ds(line, planes, stride=box.slab), :] = lined[:, column : column + 128]
    for p in range(box.blocks):
        if box.narrow is not None:
            first, last = p * stride, p * stride + box.sent * box.slab
            added = [to_ref[t, last : last + box.slab, :] for t in range(tiles)]
            added = moved(box, jnp.concatenate(added, 1), False)
            for t in range(tiles):
                to_ref[t, first : first + box.slab, :] += added[:, t * 128 : (t + 1) * 128]
        for t in range(tiles):
            out_ref[p, :, t * 128 : (t + 1) * 128] = to_ref[
                t, p * stride : p * stride + box.rows, :
            ].astype(BF16)


def gather_kernel(mine_ref, other_ref, out_ref, sems):
    rows = mine_ref.shape[0]
    copies = [
        pltpu.make_async_copy(ref, out_ref.at[n * rows : (n + 1) * rows], sems.at[n])
        for n, ref in enumerate((mine_ref, other_ref))
    ]
    for copy in copies:
        copy.start()
    for copy in copies:
        copy.wait()


def term_kernel(
    box, in_ref, row_ref, z_ref, resp_ref, factor_ref, down_y_ref, low_ref, term_ref, space_ref
):
    zpad, ypad, slab = box.zpad, box.ypad, box.slab
    for q in range(box.blocks):
        space_ref[q] = in_ref[q].astype(F32)
    fields = []
    for s in range(box.slots):
        n = 0 if s == box.narrow else box.order.index(s)
        plane = jnp.concatenate(
            [space_ref[q, n * slab : (n + 1) * slab, :] for q in range(box.blocks)], 0
        )
        if s == box.narrow:
            plane = moved(box, plane, True)
        parts = dot(down_y_ref[...], plane.astype(BF16))
        fields.append(parts[:ypad] + quarter(parts[ypad:], zpad))
    field = jnp.concatenate(fields, 0).T.astype(BF16)
    for start, size in chunks(box.count, 1024):
        span = slice(start, start + size)
        chosen = jnp.where(pick_rows(box.slots * ypad, row_ref[:, span]), 1.0, 0.0).astype(BF16)
        at_z = pick_rows(zpad, z_ref[:, span])
        found = dot(field, chosen)
        pair = resp_ref[0, :, span].astype(F32)
        rows = []
        for c in range(2):
            value = jnp.sum(jnp.where(at_z, found[c * zpad : (c + 1) * zpad], 0.0), 0, keepdims=True)
            own = (factor_ref[:, span] * pair[c : c + 1]).astype(BF16).astype(F32)
            rows.append(own + value)
        both = jnp.concatenate(rows, 0)
        term_ref[0, :, span] = both
        low_ref[0, :, span] = both.astype(BF16)


def call(kernel, out_shape, scratch, args, flops, limit, left=(), resident=(), scalars=()):
    def space(n):
        if n in left:
            return pltpu.HBM
        return pltpu.VMEM if n in resident else pltpu.SMEM if n in scalars else None

    return pl.pallas_call(
        kernel,
        out_shape=out_shape,
        in_specs=[pl.BlockSpec(memory_space=space(n)) for n in range(len(args))],
        scratch_shapes=scratch,
        compiler_params=pltpu.CompilerParams(vmem_limit_bytes=limit << 20),
        cost_estimate=pl.CostEstimate(flops=flops, bytes_accessed=4 << 20, transcendentals=0),
    )(*args)


def xor_permute(value, axis, size, distance):
    return lax.ppermute(value, axis, [(source, source ^ distance) for source in range(size)])


def sum_over(value, axis, size):
    near = 1
    while near < size:
        radix = 2 if (size // near).bit_length() % 2 == 0 else 4
        if radix == 2:
            value = value + xor_permute(value, axis, size, near)
        else:
            one, two, three = [xor_permute(value, axis, size, near * k) for k in (1, 2, 3)]
            value = (value + one) + (two + three)
        near *= radix
    return value


def on_device(sizes, response, panel, energies, offset, grid_map, potential, contact):
    rows_here, count = panel.shape[0], grid_map.shape[0]
    grid = potential.shape[0]
    bands, blocks = sizes
    box = Box(grid, blocks, count)
    down_y, up_x, down_x, up_z, down_z = box.tables()
    band_me = lax.axis_index("band")
    first_row = offset[0]

    local = first_row - band_me * rows_here
    candidates = []
    for distance in range(bands):
        row = jnp.clip(local + (band_me ^ distance), 0, rows_here - 1)
        row = lax.dynamic_slice_in_dim(panel, row, 1, 0)
        candidates.append(xor_permute(row, "band", bands, distance) if distance else row)
    owner = (first_row + band_me) // rows_here
    choice = (owner ^ band_me)[None]

    index_shape = jax.ShapeDtypeStruct((1, count), I32)
    row_index, z_index, kinetic, resp_here, up_y_here = call(
        functools.partial(index_kernel, box),
        (
            index_shape,
            index_shape,
            jax.ShapeDtypeStruct((1, count), F32),
            jax.ShapeDtypeStruct(response.shape, BF16),
            jax.ShapeDtypeStruct((grid, 2 * box.ypad), BF16),
        ),
        [],
        (grid_map, response),
        1 << 20,
        16,
    )
    shape = (blocks, box.rows, 2 * box.zpad)
    both_shape = (blocks, box.rows, 4 * box.zpad)
    field = call(
        functools.partial(scatter_kernel, box),
        jax.ShapeDtypeStruct(both_shape, BF16),
        [pltpu.VMEM(both_shape, F32)],
        (choice, row_index, z_index, resp_here, *candidates, up_y_here),
        1 << 32,
        SCATTER_LIMIT,
        (),
        range(1, 5 + bands),
        (0,),
    )
    field, panel_sent, potential, contact = lax.optimization_barrier((field, panel, potential, contact))
    potential_low, contact_low = (
        jnp.pad(jnp.transpose(value, (1, 0, 2)).astype(BF16), ((0, 0), (0, 0), (0, -grid % 128)))
        for value in (potential, contact)
    )
    beside = with_layout_constraint(xor_permute(panel_sent, "band", bands, 1), Layout((0, 1, 2)))
    shift = lax.dynamic_slice_in_dim(energies, first_row + band_me, 1, 0)
    factor = kinetic - shift[0]
    field = lax.all_to_all(field, "pw", split_axis=0, concat_axis=0, tiled=True)

    tiles, height = 2 * box.zpad // 128, blocks * box.spad * box.slab
    wide = call(
        functools.partial(x_kernel, box),
        jax.ShapeDtypeStruct((2, box.slab, grid, 2 * box.zpad), BF16),
        [pltpu.VMEM((2 * tiles, height, 128), F32)],
        (field, up_x),
        1 << 31,
        MIX_LIMIT,
        (),
        range(2),
    )
    returned = call(
        functools.partial(mix_kernel, box),
        jax.ShapeDtypeStruct(shape, BF16),
        [
            pltpu.VMEM((tiles, height, 128), F32),
            pltpu.VMEM((grid, box.slab * 2 * box.zpad), BF16),
        ],
        (wide, potential_low, contact_low, down_x, up_z, down_z),
        1 << 32,
        MIX_LIMIT,
        (),
        range(6),
    )
    returned, panel_late, beside = lax.optimization_barrier((returned, panel, beside))
    rows_both = pl.pallas_call(
        gather_kernel,
        out_shape=jax.ShapeDtypeStruct((2 * rows_here, 2, count), BF16),
        in_specs=[pl.BlockSpec(memory_space=pl.ANY)] * 2,
        out_specs=pl.BlockSpec(memory_space=pltpu.VMEM),
        scratch_shapes=[pltpu.SemaphoreType.DMA((2,))],
        compiler_params=pltpu.CompilerParams(vmem_limit_bytes=16 << 20),
        cost_estimate=pl.CostEstimate(flops=0, bytes_accessed=8 << 20, transcendentals=0),
    )(panel_late, beside)
    combed = lax.all_to_all(returned, "pw", split_axis=0, concat_axis=0, tiled=True)
    combed, rows_both = lax.optimization_barrier((combed, rows_both))
    term_low, term = call(
        functools.partial(term_kernel, box),
        (
            jax.ShapeDtypeStruct((1, 2, count), BF16),
            jax.ShapeDtypeStruct((1, 2, count), F32),
        ),
        [pltpu.VMEM(shape, F32)],
        (combed, row_index, z_index, response, factor, down_y),
        1 << 32,
        16,
    )

    far = range(2, bands, 2)
    terms = jnp.concatenate(
        [term_low] + [xor_permute(term_low, "band", bands, k) for k in far], 0
    )
    other = jnp.stack([terms[:, 1], -terms[:, 0]], axis=1)
    swapped = jnp.stack([terms, other])
    correlation = jnp.einsum("mcj,dncj->dmn", rows_both, swapped, preferred_element_type=F32)
    low = sum_over(correlation, "pw", blocks).astype(BF16)
    spread = jnp.stack([jnp.stack([low[0], -low[1]]), jnp.stack([low[1], low[0]])])
    shares = jnp.einsum("mcj,dcmn->ndj", rows_both, spread, preferred_element_type=F32)
    correction = shares[:1]
    for k, distance in enumerate(far):
        share = xor_permute(shares[k + 1 : k + 2].astype(BF16), "band", bands, distance)
        correction = correction + share.astype(F32)
    summed = term - correction
    residual = summed.astype(BF16)
    response_next = (response.astype(F32) - summed / (1.0 + kinetic)[None]).astype(BF16)
    return (residual, response_next)


def solution(mesh):
    return jax.shard_map(
        functools.partial(on_device, (mesh.shape["band"], mesh.shape["pw"])),
        mesh=mesh,
        in_specs=(
            P("band", None, "pw"),
            P("band", None, "pw"),
            P(),
            P(),
            P("pw"),
            P(None, "pw", None),
            P(None, "pw", None),
        ),
        out_specs=(P("band", None, "pw"), P("band", None, "pw")),
        check_vma=False,
    )
```

```python
import functools
import math

import jax
import jax.numpy as jnp
import numpy as np
from jax import lax
from jax.experimental import pallas as pl
from jax.experimental.layout import Layout, with_layout_constraint
from jax.experimental.pallas import tpu as pltpu
from jax.sharding import PartitionSpec as P

F32, BF16, I32 = jnp.float32, jnp.bfloat16, jnp.int32


SCATTER_LIMIT, MIX_LIMIT = 24, 16


def up(value, step):
    return -(-value // step) * step


class Box:
    def __init__(self, grid, blocks, count):
        self.grid, self.blocks, self.count = grid, blocks, count
        self.slab = grid // blocks
        folded = np.arange(grid)
        folded = np.where(folded >= grid // 2, folded - grid, folded)
        flat = np.sort((folded[:, None] ** 2 + folded[None, :] ** 2).ravel())
        used, half, limits = set(), 0, []
        for block in range(blocks):
            planes = folded[block + blocks * np.arange(self.slab)] ** 2
            radii = np.sort((planes[:, None] + flat[None, :]).ravel())
            limit = int(radii[count - 1])
            limits.append(limit)
            used |= set(np.nonzero(planes <= limit)[0].tolist())
            half = max(half, math.isqrt(limit - int(planes.min())))
        self.low = 0
        while self.low in used and self.low < self.slab:
            self.low += 1
        self.slots = self.low + len([u for u in used if u >= self.low])
        if any(u in used for u in range(self.low, self.slab - (self.slots - self.low))):
            self.low = self.slots = self.slab
        self.planes = [s if s < self.low else s + self.slab - self.slots for s in range(self.slots)]
        self.half = min(half, grid // 2 - 1) if 2 * half + 1 <= grid else grid // 2
        self.width = min(2 * self.half + 1, grid)
        self.ypad = up(self.width, 8)
        self.zpad = 64 if self.width <= 64 else up(self.width, 128)
        reach = []
        for x in self.planes:
            held = [
                math.isqrt(limit - int(folded[block + blocks * x]) ** 2)
                for block, limit in enumerate(limits)
                if int(folded[block + blocks * x]) ** 2 <= limit
            ]
            reach.append(max(held, default=0))
        narrow = int(np.argmin(reach))
        fits = self.slots > 1 and 2 * reach[narrow] + 1 <= self.zpad - self.width
        self.order = [s for s in range(self.slots) if s != narrow] + [narrow]
        self.narrow, self.reach = (narrow if fits else None), reach[narrow]
        self.turn = self.width - self.half + self.reach
        self.sent = self.slots - 1 if fits else self.slots
        self.rows = up(self.sent * self.slab, 16)
        self.spad = self.slots
        while self.spad * self.slab % 8 or self.spad * self.slab < self.rows:
            self.spad += 1

    def waves(self, first, other):
        products = (np.asarray(first)[:, None] * np.asarray(other)[None, :]) % self.grid
        angles = products.astype(np.float32) * np.float32(2.0 * math.pi / self.grid)
        scaling = np.float32(1.0 / math.sqrt(self.grid))
        return np.cos(angles) * scaling, np.sin(angles) * scaling

    def tables(self):
        grid, ypad, zpad = self.grid, self.ypad, self.zpad
        every = np.arange(grid)
        boxed = np.arange(self.width) - self.half

        def padded(part, rows, columns):
            return np.pad(part, ((0, rows - part.shape[0]), (0, columns - part.shape[1])))

        cos_y, sin_y = self.waves(every, boxed)
        down_y = np.concatenate([padded(cos_y.T, ypad, grid), padded(-sin_y.T, ypad, grid)], 0)
        cos_z, sin_z = padded(cos_y, grid, zpad), padded(sin_y, grid, zpad)
        cos_z, sin_z = (padded(part, up(grid, 128), zpad) for part in (cos_z, sin_z))
        up_z = np.stack([np.concatenate([cos_z.T, -sin_z.T], 0), np.concatenate([sin_z.T, cos_z.T], 0)])
        down_z = np.concatenate(
            [np.concatenate([cos_z, -sin_z], 1), np.concatenate([sin_z, cos_z], 1)], 0
        )
        planes = np.array([p + self.blocks * x for p in range(self.blocks) for x in (self.planes[s] for s in self.order)])
        cos_x, sin_x = self.waves(every, planes)

        def slotted(part):
            part = part.reshape(grid, self.blocks, self.slots)
            part = np.pad(part, ((0, 0), (0, 0), (0, self.spad - self.slots)))
            return part.reshape(grid, self.blocks * self.spad)

        cos_x, sin_x = slotted(cos_x), slotted(sin_x)
        up_x = np.concatenate([cos_x, sin_x], 1)
        down_x = np.concatenate([cos_x.T, -sin_x.T], 0)
        return [jnp.asarray(t, BF16) for t in (down_y, up_x, down_x, up_z, down_z)]


def quarter(field, zpad):
    pieces = []
    for start in range(0, field.shape[1], 2 * zpad):
        piece = field[:, start : start + 2 * zpad]
        if 2 * zpad == 128:
            lane = lax.broadcasted_iota(I32, piece.shape, 1)
            turned = pltpu.roll(piece, zpad, 1)
            pieces.append(jnp.where(lane < zpad, -turned, turned))
        else:
            pieces += [-piece[:, zpad:], piece[:, :zpad]]
    return pieces[0] if len(pieces) == 1 else jnp.concatenate(pieces, 1)


def moved(box, field, back):
    pieces, span = [], 2 * box.zpad
    least = box.half - box.reach if back else box.width
    for start in range(0, field.shape[1], span):
        piece = field[:, start : start + span]
        turned = pltpu.roll(piece, span - box.turn if back else box.turn, 1)
        lane = lax.broadcasted_iota(I32, piece.shape, 1)
        lane = jnp.where(lane >= box.zpad, lane - box.zpad, lane)
        inside = (lane >= least) & (lane <= least + 2 * box.reach)
        pieces.append(jnp.where(inside, turned, 0.0))
    return pieces[0] if len(pieces) == 1 else jnp.concatenate(pieces, 1)


def chunks(total, step):
    return [(start, min(step, total - start)) for start in range(0, total, step)]


def dot(left, right, dims=((1,), (0,))):
    return lax.dot_general(left, right, (dims, ((), ())), preferred_element_type=F32)


def pick_rows(rows, index):
    return lax.broadcasted_iota(I32, (rows, index.shape[1]), 0) == index


def scatter_kernel(box, choice_ref, row_ref, z_ref, resp_ref, *refs):
    *partner_refs, up_y_ref, out_ref, space_ref = refs
    zpad, ypad, slab = box.zpad, box.ypad, box.slab
    choice, total = choice_ref[0], None
    for start, size in chunks(box.count, 1024):
        span = slice(start, start + size)
        chosen = jnp.where(pick_rows(box.slots * ypad, row_ref[:, span]), 1.0, 0.0).astype(BF16)
        at_z = pick_rows(zpad, z_ref[:, span])
        partner = partner_refs[0][0, :, span].astype(F32)
        for k, ref in enumerate(partner_refs[1:]):
            partner = jnp.where(choice == k + 1, ref[0, :, span].astype(F32), partner)
        values = [
            jnp.where(at_z, pair[c : c + 1], 0.0).astype(BF16)
            for pair in (resp_ref[0, :, span].astype(F32), partner)
            for c in range(2)
        ]
        piece = dot(chosen, jnp.concatenate(values, 0), ((1,), (1,)))
        total = piece if total is None else total + piece
    added = None
    for n, s in reversed(list(enumerate(box.order))):
        plane = total[s * ypad : (s + 1) * ypad]
        both = jnp.concatenate([plane, quarter(plane, zpad)], 0).astype(BF16)
        lines = dot(up_y_ref[...], both)
        if n == box.sent:
            added = moved(box, lines, False)
            continue
        if n == 0 and added is not None:
            lines = lines + added
        for q in range(box.blocks):
            space_ref[q, n * slab : (n + 1) * slab, :] = lines[q * slab : (q + 1) * slab]
    used = box.sent * slab
    for q in range(box.blocks):
        if used < box.rows:
            space_ref[q, used:, :] = jnp.zeros((box.rows - used, space_ref.shape[2]), F32)
        out_ref[q] = space_ref[q].astype(BF16)


def folded_square(coord, grid):
    folded = jnp.where(coord >= grid // 2, coord - grid, coord)
    return folded * folded


def index_kernel(box, map_ref, resp_ref, row_ref, z_ref, kinetic_ref, resp_out, table_ref):
    grid, cell = box.grid, map_ref[...][None, :].astype(F32)
    local_x = jnp.floor((cell + 0.5) * (1.0 / (grid * grid)))
    cell = cell - local_x * (grid * grid)
    grid_y = jnp.floor((cell + 0.5) * (1.0 / grid))
    grid_z = cell - grid_y * grid
    grid_x = lax.axis_index("pw").astype(F32) + box.blocks * local_x
    squares = folded_square(grid_x, grid) + folded_square(grid_y, grid) + folded_square(grid_z, grid)
    kinetic_ref[...] = 1.5 * squares / float(grid // 2 * (grid // 2))

    def boxed(coord):
        moved = coord + box.half
        return jnp.where(moved >= grid, moved - grid, moved)

    slot = jnp.where(local_x < box.low, local_x, local_x - (box.slab - box.slots))
    row_ref[...] = (slot * box.ypad + boxed(grid_y)).astype(I32)
    z_ref[...] = boxed(grid_z).astype(I32)
    resp_out[...] = resp_ref[...]
    line = lax.broadcasted_iota(I32, table_ref.shape, 0).astype(F32)
    column = lax.broadcasted_iota(I32, table_ref.shape, 1)
    sine = column >= box.ypad
    column = jnp.where(sine, column - box.ypad, column)
    products = line * (column - box.half).astype(F32)
    products = products - jnp.floor((products + 0.5) * (1.0 / grid)) * grid
    products = jnp.where(sine, products - grid / 4, products)
    waves = jnp.cos(products * (2.0 * math.pi / grid)) * (1.0 / math.sqrt(grid))
    table_ref[...] = jnp.where(column < box.width, waves, 0.0).astype(BF16)


def spread_rows(box, in_ref, from_ref):
    stride = box.spad * box.slab
    for p in range(box.blocks):
        for t in range(from_ref.shape[0]):
            from_ref[t, p * stride : p * stride + box.rows, :] = in_ref[
                p, :, t * 128 : (t + 1) * 128
            ].astype(F32)
            if box.rows < stride:
                from_ref[t, p * stride + box.rows : (p + 1) * stride, :] = jnp.zeros(
                    (stride - box.rows, 128), F32
                )
        if box.narrow is None:
            continue
        first = p * stride + box.sent * box.slab
        neighbour = moved(box, in_ref[p].astype(F32)[: box.slab], True)
        for t in range(from_ref.shape[0]):
            from_ref[t, first : first + box.slab, :] = neighbour[:, t * 128 : (t + 1) * 128]


def along_x(box, from_ref, field, up_x_ref, wide_ref):
    zpad, planes = box.zpad, box.blocks * box.spad
    tiles = 2 * zpad // 128
    both = []
    for line in range(box.slab):
        plane = jnp.concatenate(
            [
                from_ref[field * tiles + t, pl.ds(line, planes, stride=box.slab), :]
                for t in range(tiles)
            ],
            1,
        )
        both.append(jnp.concatenate([plane, quarter(plane, zpad)], 0).astype(BF16))
    wide = dot(up_x_ref[...], jnp.concatenate(both, 1)).astype(BF16)
    for line in range(box.slab):
        wide_ref[field, line] = wide[:, line * 2 * zpad : (line + 1) * 2 * zpad]


def x_kernel(box, in_ref, up_x_ref, wide_ref, from_ref):
    spread_rows(box, in_ref, from_ref)
    for field in range(2):
        along_x(box, from_ref, field, up_x_ref, wide_ref)


def mix_kernel(
    box, wide_ref, pot_ref, con_ref, down_x_ref, up_z_ref, down_z_ref, out_ref, to_ref, back_ref
):
    zpad, stride = box.zpad, box.spad * box.slab
    planes, tiles = box.blocks * box.spad, 2 * zpad // 128
    pair = 2 if box.slab % 2 == 0 else 1
    for first in range(0, box.slab, pair):
        lines = range(first, first + pair)
        potential, contact, resp, part = (
            jnp.concatenate([ref[line] for line in lines], 0)
            for ref in (pot_ref, con_ref, wide_ref.at[0], wide_ref.at[1])
        )
        potential, contact = potential.astype(F32), contact.astype(F32)
        mixed = [
            (potential * dot(resp, up_z_ref[d]) + contact * dot(part, up_z_ref[d])).astype(BF16)
            for d in range(2)
        ]
        back = dot(jnp.concatenate(mixed, 1), down_z_ref[...]).astype(BF16)
        for n, line in enumerate(lines):
            back_ref[:, line * 2 * zpad : (line + 1) * 2 * zpad] = back[
                n * box.grid : (n + 1) * box.grid
            ]
    parts = dot(down_x_ref[...], back_ref[...])
    lined = parts[:planes] + quarter(parts[planes:], zpad)
    for line in range(box.slab):
        for t in range(tiles):
            column = (line * tiles + t) * 128
            to_ref[t, pl.ds(line, planes, stride=box.slab), :] = lined[:, column : column + 128]
    for p in range(box.blocks):
        if box.narrow is not None:
            first, last = p * stride, p * stride + box.sent * box.slab
            added = [to_ref[t, last : last + box.slab, :] for t in range(tiles)]
            added = moved(box, jnp.concatenate(added, 1), False)
            for t in range(tiles):
                to_ref[t, first : first + box.slab, :] += added[:, t * 128 : (t + 1) * 128]
        for t in range(tiles):
            out_ref[p, :, t * 128 : (t + 1) * 128] = to_ref[
                t, p * stride : p * stride + box.rows, :
            ].astype(BF16)


def gather_kernel(mine_ref, other_ref, out_ref, sems):
    rows = mine_ref.shape[0]
    copies = [
        pltpu.make_async_copy(ref, out_ref.at[n * rows : (n + 1) * rows], sems.at[n])
        for n, ref in enumerate((mine_ref, other_ref))
    ]
    for copy in copies:
        copy.start()
    for copy in copies:
        copy.wait()


def term_kernel(
    box, in_ref, row_ref, z_ref, resp_ref, factor_ref, down_y_ref, low_ref, term_ref, space_ref
):
    zpad, ypad, slab = box.zpad, box.ypad, box.slab
    for q in range(box.blocks):
        space_ref[q] = in_ref[q].astype(F32)
    fields = []
    for s in range(box.slots):
        n = 0 if s == box.narrow else box.order.index(s)
        plane = jnp.concatenate(
            [space_ref[q, n * slab : (n + 1) * slab, :] for q in range(box.blocks)], 0
        )
        if s == box.narrow:
            plane = moved(box, plane, True)
        parts = dot(down_y_ref[...], plane.astype(BF16))
        fields.append(parts[:ypad] + quarter(parts[ypad:], zpad))
    field = jnp.concatenate(fields, 0).T.astype(BF16)
    for start, size in chunks(box.count, 1024):
        span = slice(start, start + size)
        chosen = jnp.where(pick_rows(box.slots * ypad, row_ref[:, span]), 1.0, 0.0).astype(BF16)
        at_z = pick_rows(zpad, z_ref[:, span])
        found = dot(field, chosen)
        pair = resp_ref[0, :, span].astype(F32)
        rows = []
        for c in range(2):
            value = jnp.sum(jnp.where(at_z, found[c * zpad : (c + 1) * zpad], 0.0), 0, keepdims=True)
            own = (factor_ref[:, span] * pair[c : c + 1]).astype(BF16).astype(F32)
            rows.append(own + value)
        both = jnp.concatenate(rows, 0)
        term_ref[0, :, span] = both
        low_ref[0, :, span] = both.astype(BF16)


def call(kernel, out_shape, scratch, args, flops, limit, left=(), resident=(), scalars=()):
    def space(n):
        if n in left:
            return pltpu.HBM
        return pltpu.VMEM if n in resident else pltpu.SMEM if n in scalars else None

    return pl.pallas_call(
        kernel,
        out_shape=out_shape,
        in_specs=[pl.BlockSpec(memory_space=space(n)) for n in range(len(args))],
        scratch_shapes=scratch,
        compiler_params=pltpu.CompilerParams(vmem_limit_bytes=limit << 20),
        cost_estimate=pl.CostEstimate(flops=flops, bytes_accessed=4 << 20, transcendentals=0),
    )(*args)


def xor_permute(value, axis, size, distance):
    return lax.ppermute(value, axis, [(source, source ^ distance) for source in range(size)])


def sum_over(value, axis, size):
    near = 1
    while near < size:
        radix = 4 if size // near >= 4 else 2
        if radix == 2:
            value = value + xor_permute(value, axis, size, near)
        else:
            one, two, three = [xor_permute(value, axis, size, near * k) for k in (1, 2, 3)]
            value = (value + one) + (two + three)
        near *= radix
    return value


def on_device(sizes, response, panel, energies, offset, grid_map, potential, contact):
    rows_here, count = panel.shape[0], grid_map.shape[0]
    grid = potential.shape[0]
    bands, blocks = sizes
    box = Box(grid, blocks, count)
    down_y, up_x, down_x, up_z, down_z = box.tables()
    band_me = lax.axis_index("band")
    first_row = offset[0]

    local = first_row - band_me * rows_here
    candidates = []
    for distance in range(bands):
        row = jnp.clip(local + (band_me ^ distance), 0, rows_here - 1)
        row = lax.dynamic_slice_in_dim(panel, row, 1, 0)
        candidates.append(xor_permute(row, "band", bands, distance) if distance else row)
    owner = (first_row + band_me) // rows_here
    choice = (owner ^ band_me)[None]

    index_shape = jax.ShapeDtypeStruct((1, count), I32)
    row_index, z_index, kinetic, resp_here, up_y_here = call(
        functools.partial(index_kernel, box),
        (
            index_shape,
            index_shape,
            jax.ShapeDtypeStruct((1, count), F32),
            jax.ShapeDtypeStruct(response.shape, BF16),
            jax.ShapeDtypeStruct((grid, 2 * box.ypad), BF16),
        ),
        [],
        (grid_map, response),
        1 << 20,
        16,
    )
    shape = (blocks, box.rows, 2 * box.zpad)
    both_shape = (blocks, box.rows, 4 * box.zpad)
    field = call(
        functools.partial(scatter_kernel, box),
        jax.ShapeDtypeStruct(both_shape, BF16),
        [pltpu.VMEM(both_shape, F32)],
        (choice, row_index, z_index, resp_here, *candidates, up_y_here),
        1 << 32,
        SCATTER_LIMIT,
        (),
        range(1, 5 + bands),
        (0,),
    )
    field, panel_sent, potential, contact = lax.optimization_barrier((field, panel, potential, contact))
    potential_low, contact_low = (
        jnp.pad(jnp.transpose(value, (1, 0, 2)).astype(BF16), ((0, 0), (0, 0), (0, -grid % 128)))
        for value in (potential, contact)
    )
    beside = with_layout_constraint(xor_permute(panel_sent, "band", bands, 1), Layout((0, 1, 2)))
    shift = lax.dynamic_slice_in_dim(energies, first_row + band_me, 1, 0)
    factor = kinetic - shift[0]
    field = lax.all_to_all(field, "pw", split_axis=0, concat_axis=0, tiled=True)

    tiles, height = 2 * box.zpad // 128, blocks * box.spad * box.slab
    wide = call(
        functools.partial(x_kernel, box),
        jax.ShapeDtypeStruct((2, box.slab, grid, 2 * box.zpad), BF16),
        [pltpu.VMEM((2 * tiles, height, 128), F32)],
        (field, up_x),
        1 << 31,
        MIX_LIMIT,
        (),
        range(2),
    )
    returned = call(
        functools.partial(mix_kernel, box),
        jax.ShapeDtypeStruct(shape, BF16),
        [
            pltpu.VMEM((tiles, height, 128), F32),
            pltpu.VMEM((grid, box.slab * 2 * box.zpad), BF16),
        ],
        (wide, potential_low, contact_low, down_x, up_z, down_z),
        1 << 32,
        MIX_LIMIT,
        (),
        range(6),
    )
    returned, panel_late, beside = lax.optimization_barrier((returned, panel, beside))
    rows_both = pl.pallas_call(
        gather_kernel,
        out_shape=jax.ShapeDtypeStruct((2 * rows_here, 2, count), BF16),
        in_specs=[pl.BlockSpec(memory_space=pl.ANY)] * 2,
        out_specs=pl.BlockSpec(memory_space=pltpu.VMEM),
        scratch_shapes=[pltpu.SemaphoreType.DMA((2,))],
        compiler_params=pltpu.CompilerParams(vmem_limit_bytes=16 << 20),
        cost_estimate=pl.CostEstimate(flops=0, bytes_accessed=8 << 20, transcendentals=0),
    )(panel_late, beside)
    combed = lax.all_to_all(returned, "pw", split_axis=0, concat_axis=0, tiled=True)
    combed, rows_both = lax.optimization_barrier((combed, rows_both))
    term_low, term = call(
        functools.partial(term_kernel, box),
        (
            jax.ShapeDtypeStruct((1, 2, count), BF16),
            jax.ShapeDtypeStruct((1, 2, count), F32),
        ),
        [pltpu.VMEM(shape, F32)],
        (combed, row_index, z_index, response, factor, down_y),
        1 << 32,
        16,
    )

    far = range(2, bands, 2)
    terms = jnp.concatenate(
        [term_low] + [xor_permute(term_low, "band", bands, k) for k in far], 0
    )
    other = jnp.stack([terms[:, 1], -terms[:, 0]], axis=1)
    swapped = jnp.stack([terms, other])
    correlation = jnp.einsum("mcj,dncj->dmn", rows_both, swapped, preferred_element_type=F32)
    low = sum_over(correlation, "pw", blocks).astype(BF16)
    spread = jnp.stack([jnp.stack([low[0], -low[1]]), jnp.stack([low[1], low[0]])])
    shares = jnp.einsum("mcj,dcmn->ndj", rows_both, spread, preferred_element_type=F32)
    correction = shares[:1]
    for k, distance in enumerate(far):
        share = xor_permute(shares[k + 1 : k + 2].astype(BF16), "band", bands, distance)
        correction = correction + share.astype(F32)
    summed = term - correction
    residual = summed.astype(BF16)
    response_next = (response.astype(F32) - summed / (1.0 + kinetic)[None]).astype(BF16)
    return (residual, response_next)


def solution(mesh):
    return jax.shard_map(
        functools.partial(on_device, (mesh.shape["band"], mesh.shape["pw"])),
        mesh=mesh,
        in_specs=(
            P("band", None, "pw"),
            P("band", None, "pw"),
            P(),
            P(),
            P("pw"),
            P(None, "pw", None),
            P(None, "pw", None),
        ),
        out_specs=(P("band", None, "pw"), P("band", None, "pw")),
        check_vma=False,
    )
```
